256 devices in a mesh: chan: 32 (over x, z_hi, y), pos: 8 (over z_lo, core).
Axes of the slice: x: 4, y: 4, z: 8 (z_hi: 2, z_lo: 4; z = z_hi * 4 + z_lo), core: 2. Of those that a mesh axis runs over, the one named last changes fastest.
Arguments:
- patches: bfloat16 [32, 8, 512, 256], P(None, 'pos', 'chan'), may hold values from -30 to 30
- tok_weight: bfloat16 [32, 256, 1024], P('chan'), may hold values from -2 to 2
- mixing: bfloat16 [32, 16, 16], P('chan'), may hold values from -1.5 to 1.5
- chan_embed: bfloat16 [512, 1024], P('chan'), may hold values from -3 to 3
- norm_gain: float32 [1024], replicated, may hold values from 0.5 to 1.5
- qkv_weight: bfloat16 [1024, 3072], replicated, may hold values from -8 to 8
- upstream: bfloat16 [32, 8, 512, 1024], P(None, 'pos', 'chan'), may hold values from -6 to 6
Outputs:
- encoded: bfloat16 [32, 8, 512, 1024], P(None, 'pos', 'chan')
- tok_grad: float32 [8, 32, 256, 1024], P('pos', 'chan')
- mix_grad: float32 [32, 16, 16], P('chan')
- embed_grad: float32 [512, 1024], P('chan')
The draws below stay inside these ranges and needn't reach their ends.
All inputs are finite; a program needn't handle non-finite values.
Results may differ from the reference program's by a relative error of at most 0.006.
The reference program's roundings to bfloat16 on the way count: a program that leaves them out, or rounds other values in their place, can miss the bound.
Values may be sent and summed in bfloat16 or wider, within the bound.
No kernel may reach another device: no remote copies, remote signals or barrier semaphores. Data moves between devices by JAX's collectives and lax.ppermute only.
A program may use at most 128 MiB of HBM per device.

```python
import math
import jax
import jax.numpy as jnp
from jax import lax

C = 512
GROUP = 16
PIX = 256
D = 1024
HEADS = 8
HDIM = 128
GROUPS = 32
ROWS = 32
COLS = 8


def draw_patches(key, part):
    key_scale, key_own = jax.random.split(key, 2)
    chan_scale = jnp.exp(jax.random.uniform(key_scale, (1, 1, C, 1), jnp.float32, math.log(0.3), math.log(3.0)))
    drawn = jax.random.normal(key_own, (ROWS, COLS, C, PIX), jnp.float32) * chan_scale
    return jnp.clip(drawn, -30.0, 30.0).astype(jnp.bfloat16)


def draw_tok_weight(key, part):
    key_column, key_entry = jax.random.split(key, 2)
    column_scale = jnp.exp(jax.random.uniform(key_column, (GROUPS, 1, D), jnp.float32, math.log(0.3), math.log(3.0)))
    entries = jax.random.normal(key_entry, (GROUPS, PIX, D), jnp.float32)
    drawn = entries * column_scale / math.sqrt(PIX)
    return jnp.clip(drawn, -2.0, 2.0).astype(jnp.bfloat16)


def draw_qkv_weight(key, part):
    key_query, key_key, key_value = jax.random.split(key, 3)
    w_query = jax.random.normal(key_query, (D, D), jnp.float32) / math.sqrt(D)
    w_key = jax.random.normal(key_key, (D, D), jnp.float32) / math.sqrt(D)
    w_value = jax.random.normal(key_value, (D, D), jnp.float32) / math.sqrt(D)
    drawn = jnp.concatenate([w_query, w_key, w_value], axis=1)
    return jnp.clip(drawn, -8.0, 8.0).astype(jnp.bfloat16)


def block_levels(key, dims, pieces, smallest, top_value):
    level = 1.0
    for dim, blocks in pieces:
        heights = jax.random.uniform(jax.random.fold_in(jax.random.fold_in(key, 6), dim), (blocks,), jnp.float32, smallest / len(pieces), top_value / len(pieces))
        level = level * jnp.repeat(jnp.exp(heights), dims[dim] // blocks).reshape((-1,) + (1,) * (len(dims) - 1 - dim))
    return level


def scatter_about(rng, shape, scale, limit, pieces=(), held_as=jnp.bfloat16):
    factor_of = block_levels(rng, shape, pieces, -0.22, 0.18) if pieces else 1.0
    result = jax.random.normal(rng, shape, jnp.float32) * scale * factor_of
    return jnp.minimum(jnp.maximum(result, -limit), limit).astype(held_as)


def setup_inputs(seed: int = 0) -> dict:
    keys = jax.random.split(jax.random.key(seed), 8)
    patches = draw_patches(jax.random.fold_in(keys[7], 71), 0)
    tok_weight = draw_tok_weight(jax.random.fold_in(keys[7], 71), 0)
    mixing = scatter_about(keys[2], (GROUPS, GROUP, GROUP), GROUP ** -0.5, 1.5, ((0, 32),))
    chan_embed = scatter_about(keys[3], (C, D), 0.5, 3.0, ((0, 32),))
    norm_gain = jnp.clip(1.0 + 0.1 * jax.random.normal(keys[4], (D,), jnp.float32), 0.5, 1.5)
    qkv_weight = draw_qkv_weight(jax.random.fold_in(keys[7], 71), 0)
    upstream = scatter_about(keys[6], (ROWS, COLS, C, D), 1.0, 6.0, ((1, 8), (2, 32)))
    return dict(patches=patches, tok_weight=tok_weight, mixing=mixing, chan_embed=chan_embed, norm_gain=norm_gain, qkv_weight=qkv_weight, upstream=upstream)


HIGH = lax.Precision.HIGHEST

def attend_forward(mixed, qkv_weight, norm_gain):
    count, chans, width = mixed.shape
    mixed_f = mixed.astype(jnp.float32)
    inv_rms = lax.rsqrt(lax.optimization_barrier(jnp.mean(mixed_f * mixed_f, axis=-1, keepdims=True)) + 1e-06)
    normed = (mixed_f * inv_rms * norm_gain).astype(jnp.bfloat16)
    projected = jnp.dot(normed.reshape(count * chans, width), qkv_weight, preferred_element_type=jnp.float32)
    projected = projected.astype(jnp.bfloat16).reshape(count, chans, 3, HEADS, HDIM)
    queries = projected[:, :, 0]
    key_rows = projected[:, :, 1]
    values = projected[:, :, 2]
    score_scale = 1.0 / math.sqrt(HDIM)
    scores = jnp.einsum('pchd,pehd->phce', queries.astype(jnp.float32), key_rows.astype(jnp.float32), precision=HIGH) * score_scale
    row_max = lax.optimization_barrier(jnp.max(scores, axis=-1, keepdims=True))
    exp_scores = jnp.exp(scores - row_max)
    attn_probs = exp_scores / lax.optimization_barrier(jnp.sum(exp_scores, axis=-1, keepdims=True))
    probs_low = attn_probs.astype(jnp.bfloat16)
    attended = jnp.einsum('phce,pehd->pchd', probs_low.astype(jnp.float32), values.astype(jnp.float32), precision=HIGH)
    attended = attended.reshape(count, chans, width).astype(jnp.bfloat16)
    return (attended, (mixed_f, inv_rms, queries, key_rows, values, attn_probs, probs_low))

def attend_backward(saved, upstream_rows, qkv_weight, norm_gain):
    mixed_f, inv_rms, queries, key_rows, values, attn_probs, probs_low = saved
    count, chans, width = mixed_f.shape
    score_scale = 1.0 / math.sqrt(HDIM)
    grad_out = upstream_rows.reshape(count, chans, HEADS, HDIM).astype(jnp.float32)
    grad_probs = jnp.einsum('pchd,pehd->phce', grad_out, values.astype(jnp.float32), precision=HIGH)
    grad_values = jnp.einsum('phce,pchd->pehd', probs_low.astype(jnp.float32), grad_out, precision=HIGH)
    inner = lax.optimization_barrier(jnp.sum(attn_probs * grad_probs, axis=-1, keepdims=True))
    grad_scores = (attn_probs * (grad_probs - inner) * score_scale).astype(jnp.bfloat16).astype(jnp.float32)
    grad_queries = jnp.einsum('phce,pehd->pchd', grad_scores, key_rows.astype(jnp.float32), precision=HIGH)
    grad_keys = jnp.einsum('phce,pchd->pehd', grad_scores, queries.astype(jnp.float32), precision=HIGH)
    grad_projected = jnp.stack([grad_queries, grad_keys, grad_values], axis=2).astype(jnp.bfloat16)
    grad_projected = grad_projected.reshape(count * chans, 3 * width)
    grad_normed = jnp.dot(grad_projected, qkv_weight.T, preferred_element_type=jnp.float32).reshape(count, chans, width)
    scaled = grad_normed * norm_gain
    grad_branch = inv_rms * (scaled - mixed_f * inv_rms * inv_rms * lax.optimization_barrier(jnp.mean(scaled * mixed_f, axis=-1, keepdims=True)))
    return grad_branch.astype(jnp.bfloat16)

def reference(patches, tok_weight, mixing, chan_embed, norm_gain, qkv_weight, upstream):
    mixing_f = mixing.astype(jnp.float32)
    embed_f = chan_embed.astype(jnp.float32).reshape(GROUPS, GROUP, D)
    weight_f = tok_weight.astype(jnp.float32)

    def column(inputs):
        pix_col, up_col = inputs
        pix_groups = pix_col.reshape(ROWS, GROUPS, GROUP, PIX).astype(jnp.float32)
        tokens = jnp.einsum('rgcp,gpd->rgcd', pix_groups, weight_f, precision=HIGH).astype(jnp.bfloat16)
        mixed = jnp.einsum('gcf,rgfd->rgcd', mixing_f, tokens.astype(jnp.float32), precision=HIGH) + embed_f
        mixed = mixed.astype(jnp.bfloat16).reshape(ROWS, C, D)

        def position(pair):
            mixed_row, up_row = pair
            attended, saved = attend_forward(mixed_row[None], qkv_weight, norm_gain)
            grad_branch = attend_backward(saved, up_row[None], qkv_weight, norm_gain)
            return (attended[0], grad_branch[0])
        attended, grad_branch = lax.map(position, (mixed, up_col))
        encoded = (mixed.astype(jnp.float32) + attended.astype(jnp.float32)).astype(jnp.bfloat16)
        grad_mixed = (up_col.astype(jnp.float32) + grad_branch.astype(jnp.float32)).reshape(ROWS, GROUPS, GROUP, D)
        grad_tokens = jnp.einsum('gcf,rgcd->rgfd', mixing_f, grad_mixed, precision=HIGH).astype(jnp.bfloat16)
        col_tok = jnp.einsum('rgcp,rgcd->gpd', pix_groups, grad_tokens.astype(jnp.float32), precision=HIGH)
        col_mix = jnp.einsum('rgcd,rgfd->gcf', grad_mixed, tokens.astype(jnp.float32), precision=HIGH)
        col_embed = lax.optimization_barrier(jnp.sum(grad_mixed, axis=0)).reshape(C, D)
        return (encoded, col_tok, col_mix, col_embed)
    pix_cols = jnp.swapaxes(patches, 0, 1)
    up_cols = jnp.swapaxes(upstream, 0, 1)
    encoded, tok_grad, mix_parts, embed_parts = lax.map(column, (pix_cols, up_cols))
    return (jnp.swapaxes(encoded, 0, 1), tok_grad, lax.optimization_barrier(jnp.sum(mix_parts, axis=0)), lax.optimization_barrier(jnp.sum(embed_parts, axis=0)))
```

```python
import math

import jax
import jax.numpy as jnp
from jax import lax
from jax.experimental import pallas as pl
from jax.experimental.pallas import tpu as pltpu
from jax.sharding import PartitionSpec as P


GROUP = 16
HEADS = 8
HDIM = 128
PAIR = 2 * HDIM
EPS = 1e-06
SCALE = 1.0 / math.sqrt(HDIM)
F32 = jnp.float32
BF16 = jnp.bfloat16


def nn(a, b):
    return jnp.dot(a, b, preferred_element_type=F32)


def nt(a, b):
    return lax.dot_general(a, b, (((1,), (1,)), ((), ())), preferred_element_type=F32)


def block_diagonal(small, size):
    rows = lax.broadcasted_iota(jnp.int32, (size, GROUP), 0)
    cols = lax.broadcasted_iota(jnp.int32, (size, GROUP), 1)
    pick = (rows % GROUP == cols).astype(BF16)
    tiled = nt(nn(pick, small).astype(BF16), pick)
    same = (
        lax.broadcasted_iota(jnp.int32, (size, size), 0) // GROUP
        == lax.broadcasted_iota(jnp.int32, (size, size), 1) // GROUP
    )
    return jnp.where(same, tiled, 0.0).astype(BF16), pick


def mix_kernel(patches_ref, weight_ref, mixing_ref, embed_ref, tokens_ref, mixed_ref):
    size = patches_ref.shape[0]
    tokens = nn(patches_ref[...], weight_ref[...]).astype(BF16)
    tokens_ref[...] = tokens
    diag, pick = block_diagonal(mixing_ref[...], size)
    mixed_ref[...] = (nn(diag, tokens) + nn(pick, embed_ref[...])).astype(BF16)


def forward_kernel(
    mixed_ref, gain_ref, wq_ref, wk_ref, wv_ref,
    encoded_ref, q_ref, k_ref, v_ref, probs_ref, inv_ref, normed_ref,
):
    step = pl.program_id(0)

    @pl.when(step == 0)
    def _():
        mixed = mixed_ref[...].reshape(normed_ref.shape).astype(F32)
        inv = lax.rsqrt(jnp.mean(mixed * mixed, axis=-1, keepdims=True) + EPS)
        inv_ref[...] = inv
        normed_ref[...] = (mixed * inv * gain_ref[...]).astype(BF16)

    normed = normed_ref[...]
    q_ref[...] = nn(normed, wq_ref[...]).astype(BF16)
    k_ref[...] = nn(normed, wk_ref[...]).astype(BF16)
    v_ref[...] = nn(normed, wv_ref[...]).astype(BF16)
    for i in range(2):
        cols = slice(i * HDIM, (i + 1) * HDIM)
        scores = nt(k_ref[:, cols], q_ref[:, cols]) * (SCALE * math.log2(math.e))
        exps = jnp.exp2(scores - jnp.max(scores, axis=0, keepdims=True))
        probs = exps * (1.0 / jnp.sum(exps, axis=0, keepdims=True))
        probs_ref[i] = probs
        attended = nn(v_ref[:, cols].T, probs.astype(BF16)).astype(BF16).T
        base = mixed_ref[:, :, pl.ds(pl.multiple_of(step * PAIR, PAIR) + i * HDIM, HDIM)]
        base = base.reshape(attended.shape)
        encoded_ref[:, cols] = (base.astype(F32) + attended.astype(F32)).astype(BF16)


def backward_kernel(
    upstream_ref, q_ref, k_ref, v_ref, probs_ref, wq_ref, wk_ref, wv_ref,
    mixed_ref, inv_ref, gain_ref, branch_ref, gq_ref, gk_ref, gv_ref, acc_ref,
):
    step = pl.program_id(0)
    for i in range(2):
        cols = slice(i * HDIM, (i + 1) * HDIM)
        up = upstream_ref[:, :, cols].reshape(-1, HDIM)
        probs = probs_ref[i]
        grad_probs = nt(v_ref[:, cols], up)
        inner = jnp.sum(probs * grad_probs, axis=0, keepdims=True)
        grad_scores = (probs * (grad_probs - inner) * SCALE).astype(BF16)
        gv_ref[:, cols] = nn(probs.astype(BF16), up).astype(BF16)
        gk_ref[:, cols] = nn(grad_scores, q_ref[:, cols]).astype(BF16)
        gq_ref[:, cols] = nn(k_ref[:, cols].T, grad_scores).astype(BF16).T
    grad = (
        nt(gq_ref[...], wq_ref[...]) + nt(gk_ref[...], wk_ref[...]) + nt(gv_ref[...], wv_ref[...])
    )

    @pl.when(step == 0)
    def _():
        acc_ref[...] = grad

    @pl.when(step > 0)
    def _():
        acc_ref[...] += grad

    @pl.when(step == pl.num_programs(0) - 1)
    def _():
        scaled = acc_ref[...] * gain_ref[...]
        mixed = mixed_ref[...].reshape(acc_ref.shape).astype(F32)
        inv = inv_ref[...]
        mean = jnp.mean(scaled * mixed, axis=-1, keepdims=True)
        branch_ref[...] = (inv * (scaled - mixed * (inv * inv * mean))).astype(BF16)


def partial_sums(rows_ref, tokens_ref):
    count = rows_ref.shape[0]
    width = rows_ref.shape[2]
    size = 256
    per = size // GROUP
    embed = jnp.sum(rows_ref[...].astype(F32), axis=0)
    folded = jnp.zeros((GROUP, size), F32)
    same = (
        lax.broadcasted_iota(jnp.int32, (size, size), 0) // GROUP
        == lax.broadcasted_iota(jnp.int32, (size, size), 1) // GROUP
    )
    for b in range(count // per):
        tokens = tokens_ref[b * size : (b + 1) * size, :]
        rows = rows_ref[b * per : (b + 1) * per].reshape(size, width)
        prods = jnp.where(same, nt(rows, tokens), 0.0)
        folded += jnp.sum(prods.reshape(per, GROUP, size), axis=0)
    folded = folded[:, :HDIM] + folded[:, HDIM:]
    for shift in (64, 32, 16):
        folded = folded + pltpu.roll(folded, shift, 1)
    return jnp.concatenate([embed, folded], axis=1)


def side_kernel(upstream_ref, tokens_ref, patches_ref, part_ref, pixels_ref):
    part_ref[...] = partial_sums(upstream_ref, tokens_ref)
    pixels_ref[...] = patches_ref[...].T


def sums_kernel(core_ref, part_ref, branch_ref, tokens_ref, keep_ref, send_ref):
    both = part_ref[...] + partial_sums(branch_ref, tokens_ref)
    half = GROUP // 2
    first = core_ref[0] == 0
    keep_ref[...] = jnp.where(first, both[:half], both[half:])
    send_ref[...] = jnp.where(first, both[half:], both[:half])


def weight_kernel(mixing_ref, upstream_ref, branch_ref, pixels_ref, out_ref):
    step = pl.program_id(0)
    size = pixels_ref.shape[1]
    width = upstream_ref.shape[2]
    diag, _ = block_diagonal(mixing_ref[...], size)
    up = upstream_ref[...].reshape(size, width)
    branch = branch_ref[...].reshape(size, width)
    diag_t = diag.T
    grad_tokens = (nn(diag_t, up) + nn(diag_t, branch)).astype(BF16)
    part = nn(pixels_ref[...], grad_tokens)

    @pl.when(step == 0)
    def _():
        out_ref[...] = part

    @pl.when(step > 0)
    def _():
        out_ref[...] += part


def final_kernel(core_ref, mine_ref, other_ref, embed_ref, mix_ref):
    half = GROUP // 2
    width = embed_ref.shape[1]
    first = core_ref[0] == 0
    mine = mine_ref[...]
    other = other_ref[...]
    low = jnp.where(first, mine, other)
    high = jnp.where(first, other, mine)
    embed_ref[:half, :] = low[:, :width]
    embed_ref[half:, :] = high[:, :width]
    mix_ref[:half, :] = low[:, width : width + GROUP]
    mix_ref[half:, :] = high[:, width : width + GROUP]


def to_hbm(x):
    return pltpu.with_memory_space_constraint(x, pltpu.HBM)


def whole(shape):
    return pl.BlockSpec(shape, lambda *_: (0,) * len(shape))


def shape(dims, dtype):
    return jax.ShapeDtypeStruct(dims, dtype)


def cost(flops, read):
    return pl.CostEstimate(flops=flops, bytes_accessed=read, transcendentals=0)


def step(patches, tok_weight, mixing, chan_embed, norm_gain, qkv_weight, upstream):
    count = patches.shape[0]
    pix = patches.shape[3]
    width = tok_weight.shape[2]
    rows = count * GROUP
    chans = lax.axis_size("chan") * GROUP
    steps = width // PAIR
    post = (chans // GROUP, GROUP, width)
    patches = patches.reshape(rows, pix)
    tok_weight = tok_weight.reshape(pix, width)
    mixing = mixing.reshape(GROUP, GROUP)
    upstream = upstream.reshape(count, GROUP, width)
    gain = norm_gain.reshape(1, width)
    block = 256
    tokens, mixed = pl.pallas_call(
        mix_kernel,
        grid=(rows // block,),
        in_specs=[
            pl.BlockSpec((block, pix), lambda i: (i, 0)),
            whole((pix, width)),
            whole((GROUP, GROUP)),
            whole((GROUP, width)),
        ],
        out_specs=[pl.BlockSpec((block, width), lambda i: (i, 0))] * 2,
        out_shape=[shape((rows, width), BF16)] * 2,
        cost_estimate=cost(4 * rows * pix * width, 4 * rows * width),
        name="mix",
    )(patches, tok_weight, mixing, chan_embed)

    def exchange(x):
        return lax.all_to_all(x.reshape(-1, GROUP, width), "chan", 0, 0, tiled=True)

    mixed_post = to_hbm(exchange(mixed))
    upstream_post = to_hbm(exchange(upstream))
    vmem = pl.BlockSpec(memory_space=pltpu.VMEM)
    part, pixels = pl.pallas_call(
        side_kernel,
        in_specs=[vmem] * 3,
        out_specs=[vmem] * 2,
        out_shape=[shape((GROUP, width + HDIM), F32), shape((pix, rows), BF16)],
        cost_estimate=cost(2 * rows * block * width, 4 << 20),
        name="side",
    )(upstream, tokens, patches)
    column = lambda part: pl.BlockSpec((width, PAIR), lambda i: (0, part * steps + i))
    heads = pl.BlockSpec((chans, PAIR), lambda i: (0, i))
    pairs = pl.BlockSpec((2, chans, chans), lambda i: (i, 0, 0))
    encoded, q, k, v, probs, inv = pl.pallas_call(
        forward_kernel,
        grid=(steps,),
        in_specs=[whole(post), whole((1, width)), column(0), column(1), column(2)],
        out_specs=[heads, heads, heads, heads, pairs, whole((chans, 1))],
        out_shape=[shape((chans, width), BF16)] * 4
        + [shape((HEADS, chans, chans), F32), shape((chans, 1), F32)],
        scratch_shapes=[pltpu.VMEM((chans, width), BF16)],
        cost_estimate=cost(6 * chans * width * width + 4 * chans * chans * width, 16 << 20),
        name="attend_forward",
    )(mixed_post, gain, qkv_weight, qkv_weight, qkv_weight)
    encoded = exchange(encoded)
    branch = pl.pallas_call(
        backward_kernel,
        grid=(steps,),
        in_specs=[pl.BlockSpec((*post[:2], PAIR), lambda i: (0, 0, i))]
        + [heads] * 3
        + [pairs, column(0), column(1), column(2)]
        + [whole(post), whole((chans, 1)), whole((1, width))],
        out_specs=whole((chans, width)),
        out_shape=shape((chans, width), BF16),
        scratch_shapes=[pltpu.VMEM((chans, PAIR), BF16)] * 3 + [pltpu.VMEM((chans, width), F32)],
        cost_estimate=cost(6 * chans * width * width + 8 * chans * chans * width, 16 << 20),
        name="attend_backward",
    )(upstream_post, q, k, v, probs, qkv_weight, qkv_weight, qkv_weight, mixed_post, inv, gain)
    branch = to_hbm(exchange(branch))
    core = (lax.axis_index("pos") % 2).astype(jnp.int32).reshape(1)
    smem = pl.BlockSpec(memory_space=pltpu.SMEM)
    half = shape((GROUP // 2, width + HDIM), F32)
    keep, send = pl.pallas_call(
        sums_kernel,
        in_specs=[smem] + [vmem] * 3,
        out_specs=[vmem] * 2,
        out_shape=[half] * 2,
        cost_estimate=cost(2 * rows * block * width, 4 << 20),
        name="sums",
    )(core, part, branch, tokens)
    ranks = range(lax.axis_size("pos"))

    def swap(x, bit):
        return lax.ppermute(x, "pos", [(p, p ^ bit) for p in ranks])

    total = keep + swap(send, 1)
    total = (total + swap(total, 2)) + (swap(total, 4) + swap(total, 6))
    embed_grad, mix_grad = pl.pallas_call(
        final_kernel,
        in_specs=[smem] + [vmem] * 2,
        out_specs=[vmem] * 2,
        out_shape=[shape((GROUP, width), F32), shape((GROUP, GROUP), F32)],
        name="final",
    )(core, total, swap(total, 1))
    per = block // GROUP
    tok_grad = pl.pallas_call(
        weight_kernel,
        grid=(rows // block,),
        in_specs=[
            whole((GROUP, GROUP)),
            pl.BlockSpec((per, GROUP, width), lambda i: (i, 0, 0)),
            pl.BlockSpec((per, GROUP, width), lambda i: (i, 0, 0)),
            pl.BlockSpec((pix, block), lambda i: (0, i)),
        ],
        out_specs=whole((pix, width)),
        out_shape=shape((pix, width), F32),
        cost_estimate=cost(8 * rows * pix * width, 4 << 20),
        name="weight",
    )
    tok_grad = tok_grad(mixing, upstream, branch, pixels)
    return (
        encoded.reshape(count, 1, GROUP, width),
        tok_grad.reshape(1, 1, pix, width),
        mix_grad.reshape(1, GROUP, GROUP),
        embed_grad,
    )


def solution(mesh):
    in_specs = (
        P(None, "pos", "chan", None),
        P("chan", None, None),
        P("chan", None, None),
        P("chan", None),
        P(),
        P(),
        P(None, "pos", "chan", None),
    )
    out_specs = (
        P(None, "pos", "chan", None),
        P("pos", "chan", None, None),
        P("chan", None, None),
        P("chan", None),
    )
    return jax.shard_map(step, mesh=mesh, in_specs=in_specs, out_specs=out_specs, check_vma=False)
```

```python
import math

import jax
import jax.numpy as jnp
from jax import lax
from jax.experimental import pallas as pl
from jax.experimental.pallas import tpu as pltpu
from jax.sharding import PartitionSpec as P


GROUP = 16
HEADS = 8
HDIM = 128
PAIR = 2 * HDIM
EPS = 1e-06
SCALE = 1.0 / math.sqrt(HDIM)
X, HALVES, Y = 4, 2, 4
PLANE = X * Y
BASE = [x * HALVES * Y + y for x in range(X) for y in range(Y)]
F32 = jnp.float32
BF16 = jnp.bfloat16


def nn(a, b):
    return jnp.dot(a, b, preferred_element_type=F32)


def nt(a, b):
    return lax.dot_general(a, b, (((1,), (1,)), ((), ())), preferred_element_type=F32)


def block_diagonal(small, size):
    rows = lax.broadcasted_iota(jnp.int32, (size, GROUP), 0)
    cols = lax.broadcasted_iota(jnp.int32, (size, GROUP), 1)
    pick = (rows % GROUP == cols).astype(BF16)
    tiled = nt(nn(pick, small).astype(BF16), pick)
    same = (
        lax.broadcasted_iota(jnp.int32, (size, size), 0) // GROUP
        == lax.broadcasted_iota(jnp.int32, (size, size), 1) // GROUP
    )
    return jnp.where(same, tiled, 0.0).astype(BF16), pick


def mix_block(start, patches_ref, weight_ref, mixing_ref, embed_ref, tokens_ref):
    pixels = jnp.concatenate([patches_ref[base + start] for base in BASE], axis=0)
    tokens = nn(pixels, weight_ref[...]).astype(BF16)
    tokens_ref[...] = tokens
    diag, pick = block_diagonal(mixing_ref[...], tokens.shape[0])
    mixed = (nn(diag, tokens) + nn(pick, embed_ref[...])).astype(BF16)
    return mixed.reshape(PLANE, GROUP, -1)


def mix_kernel(start_ref, patches_ref, weight_ref, mixing_ref, embed_ref, tokens_ref, mixed_ref):
    mixed_ref[...] = mix_block(
        start_ref[0], patches_ref, weight_ref, mixing_ref, embed_ref, tokens_ref
    )


def mix_near_kernel(
    start_ref, patches_ref, weight_ref, mixing_ref, embed_ref, upstream_ref, tokens_ref, both_ref
):
    both_ref[:, :GROUP] = mix_block(
        start_ref[0], patches_ref, weight_ref, mixing_ref, embed_ref, tokens_ref
    )
    both_ref[:, GROUP:] = upstream_ref[...]


def pack_kernel(same_ref, other_ref, both_ref):
    both_ref[:, :GROUP] = same_ref[...]
    both_ref[:, GROUP:] = other_ref[...]


def split_kernel(same_at, other_at, upstream_ref, same_ref, other_ref):
    for k, base in enumerate(BASE):
        same_ref[k] = upstream_ref[base + same_at[0]]
        other_ref[k] = upstream_ref[base + other_at[0]]


def place_kernel(same_at, other_at, both_ref, out_ref):
    for k, base in enumerate(BASE):
        out_ref[base + same_at[0]] = both_ref[k, :GROUP]
        out_ref[base + other_at[0]] = both_ref[k, GROUP:]


def project_kernel(
    near_ref, far_ref, gain_ref, wq_ref, wk_ref, wv_ref, q_ref, k_ref, v_ref, inv_ref, normed_ref
):
    half = normed_ref.shape[0] // 2

    @pl.when(pl.program_id(0) == 0)
    def _():
        for ref, at in ((near_ref, 0), (far_ref, half)):
            mixed = ref[:, :GROUP].reshape(half, -1).astype(F32)
            inv = lax.rsqrt(jnp.mean(mixed * mixed, axis=-1, keepdims=True) + EPS)
            inv_ref[at : at + half] = inv
            normed_ref[at : at + half] = (mixed * inv * gain_ref[...]).astype(BF16)

    normed = normed_ref[...]
    q_ref[...] = nn(normed, wq_ref[...]).astype(BF16)
    k_ref[...] = nn(normed, wk_ref[...]).astype(BF16)
    v_ref[...] = nn(normed, wv_ref[...]).astype(BF16)


def forward_kernel(near_ref, far_ref, q_ref, k_ref, v_ref, first_ref, second_ref, probs_ref):
    step = pl.program_id(0)
    half = first_ref.shape[0]
    for i in range(2):
        cols = slice(i * HDIM, (i + 1) * HDIM)
        scores = nt(k_ref[:, cols], q_ref[:, cols]) * (SCALE * math.log2(math.e))
        exps = jnp.exp2(scores - jnp.max(scores, axis=0, keepdims=True))
        probs = exps * (1.0 / jnp.sum(exps, axis=0, keepdims=True))
        probs_ref[i] = probs
        attended = nn(v_ref[:, cols].T, probs.astype(BF16)).astype(BF16).T
        here = pl.ds(pl.multiple_of(step * PAIR, PAIR) + i * HDIM, HDIM)
        for ref, out_ref, at in ((near_ref, first_ref, 0), (far_ref, second_ref, half)):
            base = ref[:, :GROUP, here].reshape(half, HDIM).astype(F32)
            out_ref[:, cols] = (base + attended[at : at + half].astype(F32)).astype(BF16)


def backward_kernel(
    near_at, far_at,
    near_ref, up_far_ref, q_ref, k_ref, v_ref, probs_ref, wq_ref, wk_ref, wv_ref,
    far_ref, inv_ref, gain_ref, branch_ref, gq_ref, gk_ref, gv_ref, acc_ref,
):
    step = pl.program_id(0)
    half = acc_ref.shape[0] // 2
    for i in range(2):
        cols = slice(i * HDIM, (i + 1) * HDIM)
        here = pl.ds(pl.multiple_of(step * PAIR, PAIR) + i * HDIM, HDIM)
        up = jnp.concatenate(
            [
                near_ref[:, GROUP:, here].reshape(half, HDIM),
                up_far_ref[:, :, here].reshape(half, HDIM),
            ],
            axis=0,
        )
        probs = probs_ref[i]
        grad_probs = nt(v_ref[:, cols], up)
        inner = jnp.sum(probs * grad_probs, axis=0, keepdims=True)
        grad_scores = (probs * (grad_probs - inner) * SCALE).astype(BF16)
        gv_ref[:, cols] = nn(probs.astype(BF16), up).astype(BF16)
        gk_ref[:, cols] = nn(grad_scores, q_ref[:, cols]).astype(BF16)
        gq_ref[:, cols] = nn(k_ref[:, cols].T, grad_scores).astype(BF16).T
    grad = (
        nt(gq_ref[...], wq_ref[...]) + nt(gk_ref[...], wk_ref[...]) + nt(gv_ref[...], wv_ref[...])
    )

    @pl.when(step == 0)
    def _():
        acc_ref[...] = grad

    @pl.when(step > 0)
    def _():
        acc_ref[...] += grad

    @pl.when(step == pl.num_programs(0) - 1)
    def _():
        for ref, to, at in ((near_ref, near_at, 0), (far_ref, far_at, half)):
            scaled = acc_ref[at : at + half] * gain_ref[...]
            mixed = ref[:, :GROUP].reshape(half, -1).astype(F32)
            inv = inv_ref[at : at + half]
            mean = jnp.mean(scaled * mixed, axis=-1, keepdims=True)
            branch = (inv * (scaled - mixed * (inv * inv * mean))).astype(BF16)
            branch_ref[pl.ds(to[0], PLANE)] = branch.reshape(PLANE, GROUP, -1)


def partial_sums(rows, tokens):
    count, _, width = rows.shape
    size = count * GROUP
    embed = jnp.sum(rows.astype(F32), axis=0)
    same = (
        lax.broadcasted_iota(jnp.int32, (size, size), 0) // GROUP
        == lax.broadcasted_iota(jnp.int32, (size, size), 1) // GROUP
    )
    prods = jnp.where(same, nt(rows.reshape(size, width), tokens), 0.0)
    folded = jnp.sum(prods.reshape(count, GROUP, size), axis=0)
    folded = folded[:, :HDIM] + folded[:, HDIM:]
    for shift in (64, 32, 16):
        folded = folded + pltpu.roll(folded, shift, 1)
    return jnp.concatenate([embed, folded], axis=1)


def side_kernel(
    same_at, other_at, up_same_ref, up_other_ref, tok_same_ref, tok_other_ref, patches_ref,
    part_ref, pix_same_ref, pix_other_ref, tokens_ref,
):
    tokens_ref[: tok_same_ref.shape[0]] = tok_same_ref[...]
    tokens_ref[tok_same_ref.shape[0] :] = tok_other_ref[...]
    part_ref[...] = partial_sums(up_same_ref[...], tok_same_ref[...]) + partial_sums(
        up_other_ref[...], tok_other_ref[...]
    )
    for at, pixels_ref in ((same_at, pix_same_ref), (other_at, pix_other_ref)):
        start = at[0]
        pixels_ref[...] = jnp.concatenate([patches_ref[base + start] for base in BASE], axis=0).T


def sums_kernel(
    core_ref, near_at, far_at, part_ref, branch_ref, tokens_ref, keep_ref, send_ref
):
    both = part_ref[...]
    size = PLANE * GROUP
    for i, at in enumerate((near_at, far_at)):
        tokens = tokens_ref[i * size : (i + 1) * size]
        both += partial_sums(branch_ref[pl.ds(at[0], PLANE)], tokens)
    half = GROUP // 2
    first = core_ref[0] == 0
    keep_ref[...] = jnp.where(first, both[:half], both[half:])
    send_ref[...] = jnp.where(first, both[half:], both[:half])


def weight_kernel(
    near_at, far_at, mixing_ref, up_same_ref, up_other_ref, branch_ref, pix_same_ref,
    pix_other_ref, out_ref,
):
    size = pix_same_ref.shape[1]
    width = out_ref.shape[1]
    diag, _ = block_diagonal(mixing_ref[...], size)
    diag_t = diag.T
    total = None
    for at, up_ref, pixels_ref in (
        (near_at, up_same_ref, pix_same_ref), (far_at, up_other_ref, pix_other_ref)
    ):
        up = up_ref[...].reshape(size, width)
        branch = branch_ref[pl.ds(at[0], PLANE)].reshape(size, width)
        grad_tokens = (nn(diag_t, up) + nn(diag_t, branch)).astype(BF16)
        part = nn(pixels_ref[...], grad_tokens)
        total = part if total is None else total + part
    out_ref[...] = total


def final_kernel(core_ref, mine_ref, other_ref, embed_ref, mix_ref):
    half = GROUP // 2
    width = embed_ref.shape[1]
    first = core_ref[0] == 0
    mine = mine_ref[...]
    other = other_ref[...]
    low = jnp.where(first, mine, other)
    high = jnp.where(first, other, mine)
    embed_ref[:half, :] = low[:, :width]
    embed_ref[half:, :] = high[:, :width]
    mix_ref[:half, :] = low[:, width : width + GROUP]
    mix_ref[half:, :] = high[:, width : width + GROUP]


def to_vmem(x):
    return pltpu.with_memory_space_constraint(x, pltpu.VMEM)


def whole(shape):
    return pl.BlockSpec(shape, lambda *_: (0,) * len(shape))


def shape(dims, dtype):
    return jax.ShapeDtypeStruct(dims, dtype)


def cost(flops, read):
    return pl.CostEstimate(flops=flops, bytes_accessed=read, transcendentals=0)


def step(patches, tok_weight, mixing, chan_embed, norm_gain, qkv_weight, upstream):
    count = patches.shape[0]
    pix = patches.shape[3]
    width = tok_weight.shape[2]
    rows = PLANE * GROUP
    chans = lax.axis_size("chan") * GROUP
    steps = width // PAIR
    patches = patches.reshape(count, GROUP, pix)
    tok_weight = tok_weight.reshape(pix, width)
    mixing = mixing.reshape(GROUP, GROUP)
    upstream = upstream.reshape(count, GROUP, width)
    gain = norm_gain.reshape(1, width)
    vmem = pl.BlockSpec(memory_space=pltpu.VMEM)
    smem = pl.BlockSpec(memory_space=pltpu.SMEM)
    near = ((lax.axis_index("chan") // Y) % HALVES * Y).astype(jnp.int32).reshape(1)
    far = Y - near
    plane = [[base + h * Y for base in BASE] for h in range(HALVES)]
    piece = shape((PLANE, GROUP, width), BF16)

    def spread(x):
        x = x.reshape(PLANE, -1, width)
        return lax.all_to_all(x, "chan", 0, 0, axis_index_groups=plane, tiled=True)

    def flip(x):
        pairs = [(c, c ^ Y) for c in range(lax.axis_size("chan"))]
        return lax.ppermute(x.reshape(PLANE, GROUP, width), "chan", pairs)

    near_rank, far_rank = near // Y * PLANE, far // Y * PLANE

    tok_other, mixed_far = pl.pallas_call(
        mix_kernel,
        in_specs=[smem] + [vmem] * 4,
        out_specs=[vmem] * 2,
        out_shape=[shape((rows, width), BF16), piece],
        cost_estimate=cost(4 * rows * pix * width, 4 * rows * width),
        name="mix_other",
    )(far, patches, tok_weight, mixing, chan_embed)
    mixed_far = flip(mixed_far)
    up_same, up_other = pl.pallas_call(
        split_kernel,
        in_specs=[smem] * 2 + [vmem],
        out_specs=[vmem] * 2,
        out_shape=[piece] * 2,
        cost_estimate=cost(0, 4 << 20),
        name="split",
    )(near, far, upstream)
    up_far = flip(up_other)
    double = shape((PLANE, 2 * GROUP, width), BF16)
    tok_same, both = pl.pallas_call(
        mix_near_kernel,
        in_specs=[smem] + [vmem] * 5,
        out_specs=[vmem] * 2,
        out_shape=[shape((rows, width), BF16), double],
        cost_estimate=cost(4 * rows * pix * width, 4 * rows * width),
        name="mix_same",
    )(near, patches, tok_weight, mixing, chan_embed, up_same)
    both = spread(both)
    part, pix_same, pix_other, tokens = pl.pallas_call(
        side_kernel,
        in_specs=[smem] * 2 + [vmem] * 5,
        out_specs=[vmem] * 4,
        out_shape=[shape((GROUP, width + HDIM), F32)]
        + [shape((pix, rows), BF16)] * 2
        + [shape((chans, width), BF16)],
        cost_estimate=cost(4 * rows * rows * width, 4 << 20),
        name="side",
    )(near, far, up_same, up_other, tok_same, tok_other, patches)
    mixed_far = spread(mixed_far)
    column = lambda part: pl.BlockSpec((width, PAIR), lambda i: (0, part * steps + i))
    heads = pl.BlockSpec((chans, PAIR), lambda i: (0, i))
    half_heads = pl.BlockSpec((rows, PAIR), lambda i: (0, i))
    pairs = pl.BlockSpec((2, chans, chans), lambda i: (i, 0, 0))
    q, k, v, inv = pl.pallas_call(
        project_kernel,
        grid=(steps,),
        in_specs=[vmem, vmem, whole((1, width)), column(0), column(1), column(2)],
        out_specs=[heads, heads, heads, whole((chans, 1))],
        out_shape=[shape((chans, width), BF16)] * 3 + [shape((chans, 1), F32)],
        scratch_shapes=[pltpu.VMEM((chans, width), BF16)],
        cost_estimate=cost(6 * chans * width * width, 10 << 20),
        name="attend_project",
    )(to_vmem(both), to_vmem(mixed_far), gain, qkv_weight, qkv_weight, qkv_weight)
    up_far = spread(up_far)
    enc_same, enc_other, probs = pl.pallas_call(
        forward_kernel,
        grid=(steps,),
        in_specs=[vmem, vmem, heads, heads, heads],
        out_specs=[half_heads, half_heads, pairs],
        out_shape=[shape((rows, width), BF16)] * 2 + [shape((HEADS, chans, chans), F32)],
        cost_estimate=cost(4 * chans * chans * width, 14 << 20),
        name="attend_forward",
    )(to_vmem(both), to_vmem(mixed_far), q, k, v)
    enc_far = flip(enc_other)
    branch = pl.pallas_call(
        backward_kernel,
        grid=(steps,),
        in_specs=[smem] * 2
        + [vmem, vmem]
        + [heads] * 3
        + [pairs, column(0), column(1), column(2), vmem]
        + [whole((chans, 1)), whole((1, width))],
        out_specs=whole((count, GROUP, width)),
        out_shape=shape((count, GROUP, width), BF16),
        scratch_shapes=[pltpu.VMEM((chans, PAIR), BF16)] * 3 + [pltpu.VMEM((chans, width), F32)],
        cost_estimate=cost(6 * chans * width * width + 8 * chans * chans * width, 16 << 20),
        name="attend_backward",
    )(
        near_rank, far_rank, to_vmem(both), to_vmem(up_far), q, k, v, probs,
        qkv_weight, qkv_weight, qkv_weight, to_vmem(mixed_far), inv, gain,
    )
    order = [c for half in plane for c in half]
    branch = lax.all_to_all(branch, "chan", 0, 0, axis_index_groups=[order], tiled=True)
    encoded = pl.pallas_call(
        pack_kernel,
        in_specs=[vmem] * 2,
        out_specs=vmem,
        out_shape=double,
        cost_estimate=cost(0, 4 << 20),
        name="pack",
    )(enc_same.reshape(piece.shape), enc_far)
    encoded = spread(encoded)
    core = (lax.axis_index("pos") % 2).astype(jnp.int32).reshape(1)
    half = shape((GROUP // 2, width + HDIM), F32)
    keep, send = pl.pallas_call(
        sums_kernel,
        in_specs=[smem] * 3 + [vmem] * 3,
        out_specs=[vmem] * 2,
        out_shape=[half] * 2,
        cost_estimate=cost(2 * rows * rows * width, 4 << 20),
        name="sums",
    )(core, near_rank, far_rank, to_vmem(part), to_vmem(branch), tokens)
    ranks = range(lax.axis_size("pos"))

    def swap(x, bit):
        return lax.ppermute(x, "pos", [(p, p ^ bit) for p in ranks])

    total = keep + swap(send, 1)
    total = (total + swap(total, 2)) + (swap(total, 4) + swap(total, 6))
    embed_grad, mix_grad = pl.pallas_call(
        final_kernel,
        in_specs=[smem] + [vmem] * 2,
        out_specs=[vmem] * 2,
        out_shape=[shape((GROUP, width), F32), shape((GROUP, GROUP), F32)],
        name="final",
    )(core, to_vmem(total), to_vmem(swap(total, 1)))
    tok_grad = pl.pallas_call(
        weight_kernel,
        in_specs=[smem] * 2 + [vmem] * 6,
        out_specs=vmem,
        out_shape=shape((pix, width), F32),
        cost_estimate=cost(8 * rows * pix * width, 4 << 20),
        name="weight",
    )(near_rank, far_rank, mixing, up_same, up_other, branch, pix_same, pix_other)
    encoded = pl.pallas_call(
        place_kernel,
        in_specs=[smem] * 2 + [vmem],
        out_specs=vmem,
        out_shape=shape((count, GROUP, width), BF16),
        cost_estimate=cost(0, 4 << 20),
        name="place",
    )(near, far, to_vmem(encoded))
    return (
        encoded.reshape(count, 1, GROUP, width),
        tok_grad.reshape(1, 1, pix, width),
        mix_grad.reshape(1, GROUP, GROUP),
        embed_grad,
    )


def solution(mesh):
    in_specs = (
        P(None, "pos", "chan", None),
        P("chan", None, None),
        P("chan", None, None),
        P("chan", None),
        P(),
        P(),
        P(None, "pos", "chan", None),
    )
    out_specs = (
        P(None, "pos", "chan", None),
        P("pos", "chan", None, None),
        P("chan", None, None),
        P("chan", None),
    )
    return jax.shard_map(step, mesh=mesh, in_specs=in_specs, out_specs=out_specs, check_vma=False)
```

```python
import math

import jax
import jax.numpy as jnp
from jax import lax
from jax.experimental import pallas as pl
from jax.experimental.pallas import tpu as pltpu
from jax.sharding import PartitionSpec as P


GROUP = 16
HEADS = 8
HDIM = 128
PAIR = 2 * HDIM
EPS = 1e-06
SCALE = 1.0 / math.sqrt(HDIM)
X, HALVES, Y = 4, 2, 4
PLANE = X * Y
BASE = [x * HALVES * Y + y for x in range(X) for y in range(Y)]
F32 = jnp.float32
BF16 = jnp.bfloat16


def nn(a, b):
    return jnp.dot(a, b, preferred_element_type=F32)


def nt(a, b):
    return lax.dot_general(a, b, (((1,), (1,)), ((), ())), preferred_element_type=F32)


def block_diagonal(small, size):
    rows = lax.broadcasted_iota(jnp.int32, (size, GROUP), 0)
    cols = lax.broadcasted_iota(jnp.int32, (size, GROUP), 1)
    pick = (rows % GROUP == cols).astype(BF16)
    tiled = nt(nn(pick, small).astype(BF16), pick)
    same = (
        lax.broadcasted_iota(jnp.int32, (size, size), 0) // GROUP
        == lax.broadcasted_iota(jnp.int32, (size, size), 1) // GROUP
    )
    return jnp.where(same, tiled, 0.0).astype(BF16), pick


def mix_block(start, patches_ref, weight_ref, mixing_ref, embed_ref, tokens_ref):
    pixels = jnp.concatenate([patches_ref[base + start] for base in BASE], axis=0)
    tokens = nn(pixels, weight_ref[...]).astype(BF16)
    tokens_ref[...] = tokens
    diag, pick = block_diagonal(mixing_ref[...], tokens.shape[0])
    mixed = (nn(diag, tokens) + nn(pick, embed_ref[...])).astype(BF16)
    return mixed.reshape(PLANE, GROUP, -1)


def mix_kernel(start_ref, patches_ref, weight_ref, mixing_ref, embed_ref, tokens_ref, mixed_ref):
    mixed_ref[...] = mix_block(
        start_ref[0], patches_ref, weight_ref, mixing_ref, embed_ref, tokens_ref
    )


def mix_near_kernel(
    near_at, far_at, patches_ref, weight_ref, mixing_ref, embed_ref, upstream_ref,
    tokens_ref, sent_ref,
):
    for k, base in enumerate(BASE):
        sent_ref[k, GROUP : 2 * GROUP] = upstream_ref[base + near_at[0]]
        sent_ref[k, 2 * GROUP :] = upstream_ref[base + far_at[0]]
    sent_ref[:, :GROUP] = mix_block(
        near_at[0], patches_ref, weight_ref, mixing_ref, embed_ref, tokens_ref
    )


def pack_kernel(same_ref, other_ref, both_ref):
    both_ref[:, :GROUP] = same_ref[...]
    both_ref[:, GROUP:] = other_ref[...]


def split_kernel(same_at, other_at, upstream_ref, same_ref, other_ref):
    for k, base in enumerate(BASE):
        same_ref[k] = upstream_ref[base + same_at[0]]
        other_ref[k] = upstream_ref[base + other_at[0]]


def place_kernel(same_at, other_at, both_ref, out_ref):
    for k, base in enumerate(BASE):
        out_ref[base + same_at[0]] = both_ref[k, :GROUP]
        out_ref[base + other_at[0]] = both_ref[k, GROUP:]


def forward_kernel(
    near_ref, far_ref, gain_ref, wq_ref, wk_ref, wv_ref,
    first_ref, second_ref, q_ref, k_ref, v_ref, probs_ref, inv_ref, normed_ref,
):
    step = pl.program_id(0)
    half = first_ref.shape[0]

    @pl.when(step == 0)
    def _():
        for ref, at in ((near_ref, 0), (far_ref, half)):
            mixed = ref[:, :GROUP].reshape(half, -1).astype(F32)
            inv = lax.rsqrt(jnp.mean(mixed * mixed, axis=-1, keepdims=True) + EPS)
            inv_ref[at : at + half] = inv
            normed_ref[at : at + half] = (mixed * inv * gain_ref[...]).astype(BF16)

    normed = normed_ref[...]
    q_ref[...] = nn(normed, wq_ref[...]).astype(BF16)
    k_ref[...] = nn(normed, wk_ref[...]).astype(BF16)
    v_ref[...] = nn(normed, wv_ref[...]).astype(BF16)
    spans = [slice(i * HDIM, (i + 1) * HDIM) for i in range(2)]
    scores = [nt(k_ref[:, cols], q_ref[:, cols]) for cols in spans]
    values = [v_ref[:, cols].T for cols in spans]
    for i, cols in enumerate(spans):
        peak = jnp.max(scores[i], axis=0, keepdims=True)
        exps = jnp.exp2((scores[i] - peak) * (SCALE * math.log2(math.e)))
        probs = exps * (1.0 / jnp.sum(exps, axis=0, keepdims=True))
        probs_ref[i] = probs
        attended = nn(values[i], probs.astype(BF16)).astype(BF16).T
        here = pl.ds(pl.multiple_of(step * PAIR, PAIR) + i * HDIM, HDIM)
        for ref, out_ref, at in ((near_ref, first_ref, 0), (far_ref, second_ref, half)):
            base = ref[:, :GROUP, here].reshape(half, HDIM).astype(F32)
            out_ref[:, cols] = (base + attended[at : at + half].astype(F32)).astype(BF16)


def backward_kernel(
    near_at, far_at,
    near_ref, up_far_ref, q_ref, k_ref, v_ref, probs_ref, wq_ref, wk_ref, wv_ref,
    far_ref, inv_ref, gain_ref, branch_ref, gq_ref, gk_ref, gv_ref, acc_ref,
):
    step = pl.program_id(0)
    half = acc_ref.shape[0] // 2
    for i in range(2):
        cols = slice(i * HDIM, (i + 1) * HDIM)
        here = pl.ds(pl.multiple_of(step * PAIR, PAIR) + i * HDIM, HDIM)
        up = jnp.concatenate(
            [
                near_ref[:, GROUP : 2 * GROUP, here].reshape(half, HDIM),
                up_far_ref[:, :, here].reshape(half, HDIM),
            ],
            axis=0,
        )
        probs = probs_ref[i]
        grad_probs = nt(v_ref[:, cols], up)
        inner = jnp.sum(probs * grad_probs, axis=0, keepdims=True)
        grad_scores = (probs * (grad_probs - inner) * SCALE).astype(BF16)
        gv_ref[:, cols] = nn(probs.astype(BF16), up).astype(BF16)
        gk_ref[:, cols] = nn(grad_scores, q_ref[:, cols]).astype(BF16)
        gq_ref[:, cols] = nn(k_ref[:, cols].T, grad_scores).astype(BF16).T
    grad = (
        nt(gq_ref[...], wq_ref[...]) + nt(gk_ref[...], wk_ref[...]) + nt(gv_ref[...], wv_ref[...])
    )

    @pl.when(step == 0)
    def _():
        acc_ref[...] = grad

    @pl.when(step > 0)
    def _():
        acc_ref[...] += grad

    @pl.when(step == pl.num_programs(0) - 1)
    def _():
        for ref, to, at in ((near_ref, near_at, 0), (far_ref, far_at, half)):
            scaled = acc_ref[at : at + half] * gain_ref[...]
            mixed = ref[:, :GROUP].reshape(half, -1).astype(F32)
            inv = inv_ref[at : at + half]
            mean = jnp.mean(scaled * mixed, axis=-1, keepdims=True)
            branch = (inv * (scaled - mixed * (inv * inv * mean))).astype(BF16)
            branch_ref[pl.ds(to[0], PLANE)] = branch.reshape(PLANE, GROUP, -1)


def partial_sums(rows, tokens):
    count, _, width = rows.shape
    size = count * GROUP
    embed = jnp.sum(rows.astype(F32), axis=0)
    same = (
        lax.broadcasted_iota(jnp.int32, (size, size), 0) // GROUP
        == lax.broadcasted_iota(jnp.int32, (size, size), 1) // GROUP
    )
    prods = jnp.where(same, nt(rows.reshape(size, width), tokens), 0.0)
    folded = jnp.sum(prods.reshape(count, GROUP, size), axis=0)
    folded = folded[:, :HDIM] + folded[:, HDIM:]
    for shift in (64, 32, 16):
        folded = folded + pltpu.roll(folded, shift, 1)
    return jnp.concatenate([embed, folded], axis=1)


def side_kernel(
    same_at, other_at, up_same_ref, up_other_ref, tok_same_ref, tok_other_ref, patches_ref,
    part_ref, pix_same_ref, pix_other_ref, tokens_ref,
):
    tokens_ref[: tok_same_ref.shape[0]] = tok_same_ref[...]
    tokens_ref[tok_same_ref.shape[0] :] = tok_other_ref[...]
    part_ref[...] = partial_sums(up_same_ref[...], tok_same_ref[...]) + partial_sums(
        up_other_ref[...], tok_other_ref[...]
    )
    for at, pixels_ref in ((same_at, pix_same_ref), (other_at, pix_other_ref)):
        start = at[0]
        pixels_ref[...] = jnp.concatenate([patches_ref[base + start] for base in BASE], axis=0).T


def sums_kernel(
    core_ref, near_at, far_at, part_ref, branch_ref, tokens_ref, keep_ref, send_ref
):
    both = part_ref[...]
    size = PLANE * GROUP
    for i, at in enumerate((near_at, far_at)):
        tokens = tokens_ref[i * size : (i + 1) * size]
        both += partial_sums(branch_ref[pl.ds(at[0], PLANE)], tokens)
    half = GROUP // 2
    first = core_ref[0] == 0
    keep_ref[...] = jnp.where(first, both[:half], both[half:])
    send_ref[...] = jnp.where(first, both[half:], both[:half])


def weight_kernel(
    near_at, far_at, mixing_ref, up_same_ref, up_other_ref, branch_ref, pix_same_ref,
    pix_other_ref, out_ref,
):
    size = pix_same_ref.shape[1]
    width = out_ref.shape[1]
    diag, _ = block_diagonal(mixing_ref[...], size)
    diag_t = diag.T
    total = None
    for at, up_ref, pixels_ref in (
        (near_at, up_same_ref, pix_same_ref), (far_at, up_other_ref, pix_other_ref)
    ):
        up = up_ref[...].reshape(size, width)
        branch = branch_ref[pl.ds(at[0], PLANE)].reshape(size, width)
        grad_tokens = (nn(diag_t, up) + nn(diag_t, branch)).astype(BF16)
        part = nn(pixels_ref[...], grad_tokens)
        total = part if total is None else total + part
    out_ref[...] = total


def final_kernel(core_ref, mine_ref, other_ref, embed_ref, mix_ref):
    half = GROUP // 2
    width = embed_ref.shape[1]
    first = core_ref[0] == 0
    mine = mine_ref[...]
    other = other_ref[...]
    low = jnp.where(first, mine, other)
    high = jnp.where(first, other, mine)
    embed_ref[:half, :] = low[:, :width]
    embed_ref[half:, :] = high[:, :width]
    mix_ref[:half, :] = low[:, width : width + GROUP]
    mix_ref[half:, :] = high[:, width : width + GROUP]


def to_vmem(x):
    return pltpu.with_memory_space_constraint(x, pltpu.VMEM)


def whole(shape):
    return pl.BlockSpec(shape, lambda *_: (0,) * len(shape))


def shape(dims, dtype):
    return jax.ShapeDtypeStruct(dims, dtype)


def cost(flops, read):
    return pl.CostEstimate(flops=flops, bytes_accessed=read, transcendentals=0)


def step(patches, tok_weight, mixing, chan_embed, norm_gain, qkv_weight, upstream):
    count = patches.shape[0]
    pix = patches.shape[3]
    width = tok_weight.shape[2]
    rows = PLANE * GROUP
    chans = lax.axis_size("chan") * GROUP
    steps = width // PAIR
    patches = patches.reshape(count, GROUP, pix)
    tok_weight = tok_weight.reshape(pix, width)
    mixing = mixing.reshape(GROUP, GROUP)
    upstream = upstream.reshape(count, GROUP, width)
    gain = norm_gain.reshape(1, width)
    vmem = pl.BlockSpec(memory_space=pltpu.VMEM)
    smem = pl.BlockSpec(memory_space=pltpu.SMEM)
    near = ((lax.axis_index("chan") // Y) % HALVES * Y).astype(jnp.int32).reshape(1)
    far = Y - near
    plane = [[base + h * Y for base in BASE] for h in range(HALVES)]
    piece = shape((PLANE, GROUP, width), BF16)

    def spread(x):
        x = x.reshape(PLANE, -1, width)
        return lax.all_to_all(x, "chan", 0, 0, axis_index_groups=plane, tiled=True)

    def flip(x):
        pairs = [(c, c ^ Y) for c in range(lax.axis_size("chan"))]
        return lax.ppermute(x.reshape(PLANE, GROUP, width), "chan", pairs)

    near_rank, far_rank = near // Y * PLANE, far // Y * PLANE

    tok_other, mixed_far = pl.pallas_call(
        mix_kernel,
        in_specs=[smem] + [vmem] * 4,
        out_specs=[vmem] * 2,
        out_shape=[shape((rows, width), BF16), piece],
        cost_estimate=cost(4 * rows * pix * width, 4 * rows * width),
        name="mix_other",
    )(far, patches, tok_weight, mixing, chan_embed)
    mixed_far = flip(mixed_far)
    tok_same, sent = pl.pallas_call(
        mix_near_kernel,
        in_specs=[smem] * 2 + [vmem] * 5,
        out_specs=[vmem] * 2,
        out_shape=[shape((rows, width), BF16), shape((PLANE, 3 * GROUP, width), BF16)],
        cost_estimate=cost(4 * rows * pix * width, 4 * rows * width),
        name="mix_same",
    )(near, far, patches, tok_weight, mixing, chan_embed, upstream)
    near_post = spread(sent)
    up_same, up_other = pl.pallas_call(
        split_kernel,
        in_specs=[smem] * 2 + [vmem],
        out_specs=[vmem] * 2,
        out_shape=[piece] * 2,
        cost_estimate=cost(0, 4 << 20),
        name="split",
    )(near, far, upstream)
    part, pix_same, pix_other, tokens = pl.pallas_call(
        side_kernel,
        in_specs=[smem] * 2 + [vmem] * 5,
        out_specs=[vmem] * 4,
        out_shape=[shape((GROUP, width + HDIM), F32)]
        + [shape((pix, rows), BF16)] * 2
        + [shape((chans, width), BF16)],
        cost_estimate=cost(4 * rows * rows * width, 4 << 20),
        name="side",
    )(near, far, up_same, up_other, tok_same, tok_other, patches)
    up_far = flip(near_post[:, 2 * GROUP :])
    mixed_far = spread(mixed_far)
    column = lambda part: pl.BlockSpec((width, PAIR), lambda i: (0, part * steps + i))
    heads = pl.BlockSpec((chans, PAIR), lambda i: (0, i))
    half_heads = pl.BlockSpec((rows, PAIR), lambda i: (0, i))
    pairs = pl.BlockSpec((2, chans, chans), lambda i: (i, 0, 0))
    enc_same, enc_other, q, k, v, probs, inv = pl.pallas_call(
        forward_kernel,
        grid=(steps,),
        in_specs=[vmem, vmem, whole((1, width)), column(0), column(1), column(2)],
        out_specs=[half_heads, half_heads, heads, heads, heads, pairs, whole((chans, 1))],
        out_shape=[shape((rows, width), BF16)] * 2
        + [shape((chans, width), BF16)] * 3
        + [shape((HEADS, chans, chans), F32), shape((chans, 1), F32)],
        scratch_shapes=[pltpu.VMEM((chans, width), BF16)],
        cost_estimate=cost(6 * chans * width * width + 4 * chans * chans * width, 16 << 20),
        name="attend_forward",
    )(to_vmem(near_post), to_vmem(mixed_far), gain, qkv_weight, qkv_weight, qkv_weight)
    enc_far = flip(enc_other)
    branch = pl.pallas_call(
        backward_kernel,
        grid=(steps,),
        in_specs=[smem] * 2
        + [vmem, vmem]
        + [heads] * 3
        + [pairs, column(0), column(1), column(2), vmem]
        + [whole((chans, 1)), whole((1, width))],
        out_specs=whole((count, GROUP, width)),
        out_shape=shape((count, GROUP, width), BF16),
        scratch_shapes=[pltpu.VMEM((chans, PAIR), BF16)] * 3 + [pltpu.VMEM((chans, width), F32)],
        cost_estimate=cost(6 * chans * width * width + 8 * chans * chans * width, 16 << 20),
        name="attend_backward",
    )(
        near_rank, far_rank, to_vmem(near_post), to_vmem(up_far), q, k, v, probs,
        qkv_weight, qkv_weight, qkv_weight, to_vmem(mixed_far), inv, gain,
    )
    order = [c for half in plane for c in half]
    branch = lax.all_to_all(branch, "chan", 0, 0, axis_index_groups=[order], tiled=True)
    double = shape((PLANE, 2 * GROUP, width), BF16)
    encoded = pl.pallas_call(
        pack_kernel,
        in_specs=[vmem] * 2,
        out_specs=vmem,
        out_shape=double,
        cost_estimate=cost(0, 4 << 20),
        name="pack",
    )(enc_same.reshape(piece.shape), enc_far)
    encoded = spread(encoded)
    core = (lax.axis_index("pos") % 2).astype(jnp.int32).reshape(1)
    half = shape((GROUP // 2, width + HDIM), F32)
    keep, send = pl.pallas_call(
        sums_kernel,
        in_specs=[smem] * 3 + [vmem] * 3,
        out_specs=[vmem] * 2,
        out_shape=[half] * 2,
        cost_estimate=cost(2 * rows * rows * width, 4 << 20),
        name="sums",
    )(core, near_rank, far_rank, to_vmem(part), to_vmem(branch), tokens)
    ranks = range(lax.axis_size("pos"))

    def swap(x, bit):
        return lax.ppermute(x, "pos", [(p, p ^ bit) for p in ranks])

    total = keep + swap(send, 1)
    total = (total + swap(total, 2)) + (swap(total, 4) + swap(total, 6))
    embed_grad, mix_grad = pl.pallas_call(
        final_kernel,
        in_specs=[smem] + [vmem] * 2,
        out_specs=[vmem] * 2,
        out_shape=[shape((GROUP, width), F32), shape((GROUP, GROUP), F32)],
        name="final",
    )(core, to_vmem(total), to_vmem(swap(total, 1)))
    tok_grad = pl.pallas_call(
        weight_kernel,
        in_specs=[smem] * 2 + [vmem] * 6,
        out_specs=vmem,
        out_shape=shape((pix, width), F32),
        cost_estimate=cost(8 * rows * pix * width, 4 << 20),
        name="weight",
    )(near_rank, far_rank, mixing, up_same, up_other, branch, pix_same, pix_other)
    encoded = pl.pallas_call(
        place_kernel,
        in_specs=[smem] * 2 + [vmem],
        out_specs=vmem,
        out_shape=shape((count, GROUP, width), BF16),
        cost_estimate=cost(0, 4 << 20),
        name="place",
    )(near, far, to_vmem(encoded))
    return (
        encoded.reshape(count, 1, GROUP, width),
        tok_grad.reshape(1, 1, pix, width),
        mix_grad.reshape(1, GROUP, GROUP),
        embed_grad,
    )


def solution(mesh):
    in_specs = (
        P(None, "pos", "chan", None),
        P("chan", None, None),
        P("chan", None, None),
        P("chan", None),
        P(),
        P(),
        P(None, "pos", "chan", None),
    )
    out_specs = (
        P(None, "pos", "chan", None),
        P("pos", "chan", None, None),
        P("chan", None, None),
        P("chan", None),
    )
    return jax.shard_map(step, mesh=mesh, in_specs=in_specs, out_specs=out_specs, check_vma=False)
```

```python
import math

import jax
import jax.numpy as jnp
from jax import lax
from jax.experimental import pallas as pl
from jax.experimental.pallas import tpu as pltpu
from jax.sharding import PartitionSpec as P


GROUP = 16
HEADS = 8
HDIM = 128
PAIR = 2 * HDIM
EPS = 1e-06
SCALE = 1.0 / math.sqrt(HDIM)
X, HALVES, Y = 4, 2, 4
PLANE = X * Y
BASE = [x * HALVES * Y + y for x in range(X) for y in range(Y)]
LIMIT = pltpu.CompilerParams(vmem_limit_bytes=58 << 20)
F32 = jnp.float32
BF16 = jnp.bfloat16


def nn(a, b):
    return jnp.dot(a, b, preferred_element_type=F32)


def nt(a, b):
    return lax.dot_general(a, b, (((1,), (1,)), ((), ())), preferred_element_type=F32)


def block_diagonal(small, size):
    rows = lax.broadcasted_iota(jnp.int32, (size, GROUP), 0)
    cols = lax.broadcasted_iota(jnp.int32, (size, GROUP), 1)
    pick = (rows % GROUP == cols).astype(BF16)
    tiled = nt(nn(pick, small).astype(BF16), pick)
    same = (
        lax.broadcasted_iota(jnp.int32, (size, size), 0) // GROUP
        == lax.broadcasted_iota(jnp.int32, (size, size), 1) // GROUP
    )
    return jnp.where(same, tiled, 0.0).astype(BF16), pick


def mix_block(start, patches_ref, weight_ref, mixing_ref, embed_ref, tokens_ref):
    pixels = jnp.concatenate([patches_ref[base + start] for base in BASE], axis=0)
    tokens = nn(pixels, weight_ref[...]).astype(BF16)
    tokens_ref[...] = tokens
    diag, pick = block_diagonal(mixing_ref[...], tokens.shape[0])
    mixed = (nn(diag, tokens) + nn(pick, embed_ref[...])).astype(BF16)
    return mixed.reshape(PLANE, GROUP, -1)


def mix_kernel(start_ref, patches_ref, weight_ref, mixing_ref, embed_ref, tokens_ref, mixed_ref):
    mixed_ref[...] = mix_block(
        start_ref[0], patches_ref, weight_ref, mixing_ref, embed_ref, tokens_ref
    )


def mix_near_kernel(
    near_at, far_at, patches_ref, weight_ref, mixing_ref, embed_ref, upstream_ref,
    tokens_ref, sent_ref,
):
    for k, base in enumerate(BASE):
        sent_ref[k, GROUP:] = upstream_ref[base + far_at[0]]
    sent_ref[:, :GROUP] = mix_block(
        near_at[0], patches_ref, weight_ref, mixing_ref, embed_ref, tokens_ref
    )


def pack_kernel(same_ref, other_ref, both_ref):
    both_ref[:, :GROUP] = same_ref[...]
    both_ref[:, GROUP:] = other_ref[...]


def split_kernel(same_at, other_at, upstream_ref, same_ref, other_ref):
    for k, base in enumerate(BASE):
        same_ref[k] = upstream_ref[base + same_at[0]]
        other_ref[k] = upstream_ref[base + other_at[0]]


def place_kernel(same_at, other_at, both_ref, out_ref):
    for k, base in enumerate(BASE):
        out_ref[base + same_at[0]] = both_ref[k, :GROUP]
        out_ref[base + other_at[0]] = both_ref[k, GROUP:]


def forward_kernel(
    near_ref, far_ref, gain_ref, wq_ref, wk_ref, wv_ref,
    first_ref, second_ref, q_ref, k_ref, v_ref, probs_ref, inv_ref, normed_ref,
):
    step = pl.program_id(0)
    half = first_ref.shape[0]

    @pl.when(step == 0)
    def _():
        for ref, at in ((near_ref, 0), (far_ref, half)):
            mixed = ref[:, :GROUP].reshape(half, -1).astype(F32)
            inv = lax.rsqrt(jnp.mean(mixed * mixed, axis=-1, keepdims=True) + EPS)
            inv_ref[at : at + half] = inv
            normed_ref[at : at + half] = (mixed * inv * gain_ref[...]).astype(BF16)

    normed = normed_ref[...]
    q_ref[...] = nn(normed, wq_ref[...]).astype(BF16)
    k_ref[...] = nn(normed, wk_ref[...]).astype(BF16)
    v_ref[...] = nn(normed, wv_ref[...]).astype(BF16)
    spans = [slice(i * HDIM, (i + 1) * HDIM) for i in range(2)]
    scores = [nt(k_ref[:, cols], q_ref[:, cols]) for cols in spans]
    values = [v_ref[:, cols].T for cols in spans]
    for i, cols in enumerate(spans):
        peak = jnp.max(scores[i], axis=0, keepdims=True)
        exps = jnp.exp2((scores[i] - peak) * (SCALE * math.log2(math.e)))
        probs = exps * (1.0 / jnp.sum(exps, axis=0, keepdims=True))
        probs_ref[i] = probs
        attended = nn(values[i], probs.astype(BF16)).astype(BF16).T
        here = pl.ds(pl.multiple_of(step * PAIR, PAIR) + i * HDIM, HDIM)
        for ref, out_ref, at in ((near_ref, first_ref, 0), (far_ref, second_ref, half)):
            base = ref[:, :GROUP, here].reshape(half, HDIM).astype(F32)
            out_ref[:, cols] = (base + attended[at : at + half].astype(F32)).astype(BF16)


def backward_kernel(
    near_at, far_at,
    near_ref, up_far_ref, q_ref, k_ref, v_ref, probs_ref, wq_ref, wk_ref, wv_ref,
    far_ref, inv_ref, gain_ref, branch_ref, gq_ref, gk_ref, gv_ref, acc_ref,
):
    step = pl.program_id(0)
    half = acc_ref.shape[0] // 2
    for i in range(2):
        cols = slice(i * HDIM, (i + 1) * HDIM)
        here = pl.ds(pl.multiple_of(step * PAIR, PAIR) + i * HDIM, HDIM)
        up = jnp.concatenate(
            [
                far_ref[:, GROUP:, here].reshape(half, HDIM),
                up_far_ref[:, :, here].reshape(half, HDIM),
            ],
            axis=0,
        )
        probs = probs_ref[i]
        grad_probs = nt(v_ref[:, cols], up)
        inner = jnp.sum(probs * grad_probs, axis=0, keepdims=True)
        grad_scores = (probs * (grad_probs - inner) * SCALE).astype(BF16)
        gv_ref[:, cols] = nn(probs.astype(BF16), up).astype(BF16)
        gk_ref[:, cols] = nn(grad_scores, q_ref[:, cols]).astype(BF16)
        gq_ref[:, cols] = nn(k_ref[:, cols].T, grad_scores).astype(BF16).T
    grad = (
        nt(gq_ref[...], wq_ref[...]) + nt(gk_ref[...], wk_ref[...]) + nt(gv_ref[...], wv_ref[...])
    )

    @pl.when(step == 0)
    def _():
        acc_ref[...] = grad

    @pl.when(step > 0)
    def _():
        acc_ref[...] += grad

    @pl.when(step == pl.num_programs(0) - 1)
    def _():
        for ref, to, at in ((near_ref, near_at, 0), (far_ref, far_at, half)):
            scaled = acc_ref[at : at + half] * gain_ref[...]
            mixed = ref[:, :GROUP].reshape(half, -1).astype(F32)
            inv = inv_ref[at : at + half]
            mean = jnp.mean(scaled * mixed, axis=-1, keepdims=True)
            branch = (inv * (scaled - mixed * (inv * inv * mean))).astype(BF16)
            branch_ref[pl.ds(to[0], PLANE)] = branch.reshape(PLANE, GROUP, -1)


def partial_sums(rows, tokens):
    count, _, width = rows.shape
    size = count * GROUP
    embed = jnp.sum(rows.astype(F32), axis=0)
    same = (
        lax.broadcasted_iota(jnp.int32, (size, size), 0) // GROUP
        == lax.broadcasted_iota(jnp.int32, (size, size), 1) // GROUP
    )
    prods = jnp.where(same, nt(rows.reshape(size, width), tokens), 0.0)
    folded = jnp.sum(prods.reshape(count, GROUP, size), axis=0)
    folded = folded[:, :HDIM] + folded[:, HDIM:]
    for shift in (64, 32, 16):
        folded = folded + pltpu.roll(folded, shift, 1)
    return jnp.concatenate([embed, folded], axis=1)


def side_kernel(
    same_at, other_at, up_same_ref, up_other_ref, tok_same_ref, tok_other_ref, patches_ref,
    part_ref, pix_same_ref, pix_other_ref, tokens_ref,
):
    tokens_ref[: tok_same_ref.shape[0]] = tok_same_ref[...]
    tokens_ref[tok_same_ref.shape[0] :] = tok_other_ref[...]
    part_ref[...] = partial_sums(up_same_ref[...], tok_same_ref[...]) + partial_sums(
        up_other_ref[...], tok_other_ref[...]
    )
    for at, pixels_ref in ((same_at, pix_same_ref), (other_at, pix_other_ref)):
        start = at[0]
        pixels_ref[...] = jnp.concatenate([patches_ref[base + start] for base in BASE], axis=0).T


def sums_kernel(
    core_ref, near_at, far_at, part_ref, branch_ref, tokens_ref, keep_ref, send_ref
):
    both = part_ref[...]
    size = PLANE * GROUP
    for i, at in enumerate((near_at, far_at)):
        tokens = tokens_ref[i * size : (i + 1) * size]
        both += partial_sums(branch_ref[pl.ds(at[0], PLANE)], tokens)
    half = GROUP // 2
    first = core_ref[0] == 0
    keep_ref[...] = jnp.where(first, both[:half], both[half:])
    send_ref[...] = jnp.where(first, both[half:], both[:half])


def weight_kernel(
    near_at, far_at, mixing_ref, up_same_ref, up_other_ref, branch_ref, pix_same_ref,
    pix_other_ref, out_ref,
):
    size = pix_same_ref.shape[1]
    width = out_ref.shape[1]
    diag, _ = block_diagonal(mixing_ref[...], size)
    diag_t = diag.T
    total = None
    for at, up_ref, pixels_ref in (
        (near_at, up_same_ref, pix_same_ref), (far_at, up_other_ref, pix_other_ref)
    ):
        up = up_ref[...].reshape(size, width)
        branch = branch_ref[pl.ds(at[0], PLANE)].reshape(size, width)
        grad_tokens = (nn(diag_t, up) + nn(diag_t, branch)).astype(BF16)
        part = nn(pixels_ref[...], grad_tokens)
        total = part if total is None else total + part
    out_ref[...] = total


def final_kernel(core_ref, mine_ref, other_ref, embed_ref, mix_ref):
    half = GROUP // 2
    width = embed_ref.shape[1]
    first = core_ref[0] == 0
    mine = mine_ref[...]
    other = other_ref[...]
    low = jnp.where(first, mine, other)
    high = jnp.where(first, other, mine)
    embed_ref[:half, :] = low[:, :width]
    embed_ref[half:, :] = high[:, :width]
    mix_ref[:half, :] = low[:, width : width + GROUP]
    mix_ref[half:, :] = high[:, width : width + GROUP]


def to_vmem(x):
    return pltpu.with_memory_space_constraint(x, pltpu.VMEM)


def whole(shape):
    return pl.BlockSpec(shape, lambda *_: (0,) * len(shape))


def shape(dims, dtype):
    return jax.ShapeDtypeStruct(dims, dtype)


def cost(flops, read):
    return pl.CostEstimate(flops=flops, bytes_accessed=read, transcendentals=0)


def step(patches, tok_weight, mixing, chan_embed, norm_gain, qkv_weight, upstream):
    count = patches.shape[0]
    pix = patches.shape[3]
    width = tok_weight.shape[2]
    rows = PLANE * GROUP
    chans = lax.axis_size("chan") * GROUP
    steps = width // PAIR
    patches = patches.reshape(count, GROUP, pix)
    tok_weight = tok_weight.reshape(pix, width)
    mixing = mixing.reshape(GROUP, GROUP)
    upstream = upstream.reshape(count, GROUP, width)
    gain = norm_gain.reshape(1, width)
    vmem = pl.BlockSpec(memory_space=pltpu.VMEM)
    smem = pl.BlockSpec(memory_space=pltpu.SMEM)
    near = ((lax.axis_index("chan") // Y) % HALVES * Y).astype(jnp.int32).reshape(1)
    far = Y - near
    plane = [[base + h * Y for base in BASE] for h in range(HALVES)]
    piece = shape((PLANE, GROUP, width), BF16)

    def spread(x):
        x = x.reshape(PLANE, -1, width)
        return lax.all_to_all(x, "chan", 0, 0, axis_index_groups=plane, tiled=True)

    def flip(x):
        pairs = [(c, c ^ Y) for c in range(lax.axis_size("chan"))]
        return lax.ppermute(x.reshape(PLANE, GROUP, width), "chan", pairs)

    near_rank, far_rank = near // Y * PLANE, far // Y * PLANE

    tok_other, mixed_far = pl.pallas_call(
        mix_kernel,
        in_specs=[smem] + [vmem] * 4,
        out_specs=[vmem] * 2,
        out_shape=[shape((rows, width), BF16), piece],
        cost_estimate=cost(4 * rows * pix * width, 4 * rows * width),
        name="mix_other",
    )(far, patches, tok_weight, mixing, chan_embed)
    mixed_far = flip(mixed_far)
    double = shape((PLANE, 2 * GROUP, width), BF16)
    tok_same, sent = pl.pallas_call(
        mix_near_kernel,
        in_specs=[smem] * 2 + [vmem] * 5,
        out_specs=[vmem] * 2,
        out_shape=[shape((rows, width), BF16), double],
        cost_estimate=cost(4 * rows * pix * width, 4 * rows * width),
        name="mix_same",
    )(near, far, patches, tok_weight, mixing, chan_embed, upstream)
    near_post = spread(sent)
    up_same, up_other = pl.pallas_call(
        split_kernel,
        in_specs=[smem] * 2 + [vmem],
        out_specs=[vmem] * 2,
        out_shape=[piece] * 2,
        cost_estimate=cost(0, 4 << 20),
        name="split",
    )(near, far, upstream)
    part, pix_same, pix_other, tokens = pl.pallas_call(
        side_kernel,
        in_specs=[smem] * 2 + [vmem] * 5,
        out_specs=[vmem] * 4,
        out_shape=[shape((GROUP, width + HDIM), F32)]
        + [shape((pix, rows), BF16)] * 2
        + [shape((chans, width), BF16)],
        cost_estimate=cost(4 * rows * rows * width, 4 << 20),
        name="side",
    )(near, far, up_same, up_other, tok_same, tok_other, patches)
    up_far = flip(near_post[:, GROUP:])

    def pack(first, second):
        return pl.pallas_call(
            pack_kernel,
            in_specs=[vmem] * 2,
            out_specs=vmem,
            out_shape=double,
            cost_estimate=cost(0, 4 << 20),
            compiler_params=LIMIT,
        )(first.reshape(piece.shape), second.reshape(piece.shape))

    far_post = spread(pack(mixed_far, up_same))
    column = lambda part: pl.BlockSpec((width, PAIR), lambda i: (0, part * steps + i))
    heads = pl.BlockSpec((chans, PAIR), lambda i: (0, i))
    half_heads = pl.BlockSpec((rows, PAIR), lambda i: (0, i))
    pairs = pl.BlockSpec((2, chans, chans), lambda i: (i, 0, 0))
    enc_same, enc_other, q, k, v, probs, inv = pl.pallas_call(
        forward_kernel,
        grid=(steps,),
        in_specs=[vmem, vmem, whole((1, width)), column(0), column(1), column(2)],
        out_specs=[half_heads, half_heads, heads, heads, heads, pairs, whole((chans, 1))],
        out_shape=[shape((rows, width), BF16)] * 2
        + [shape((chans, width), BF16)] * 3
        + [shape((HEADS, chans, chans), F32), shape((chans, 1), F32)],
        scratch_shapes=[pltpu.VMEM((chans, width), BF16)],
        cost_estimate=cost(6 * chans * width * width + 4 * chans * chans * width, 16 << 20),
        compiler_params=LIMIT,
        name="attend_forward",
    )(to_vmem(near_post), to_vmem(far_post), gain, qkv_weight, qkv_weight, qkv_weight)
    enc_far = flip(enc_other)
    branch = pl.pallas_call(
        backward_kernel,
        grid=(steps,),
        in_specs=[smem] * 2
        + [vmem, vmem]
        + [heads] * 3
        + [pairs, column(0), column(1), column(2), vmem]
        + [whole((chans, 1)), whole((1, width))],
        out_specs=whole((count, GROUP, width)),
        out_shape=shape((count, GROUP, width), BF16),
        scratch_shapes=[pltpu.VMEM((chans, PAIR), BF16)] * 3 + [pltpu.VMEM((chans, width), F32)],
        cost_estimate=cost(6 * chans * width * width + 8 * chans * chans * width, 16 << 20),
        compiler_params=LIMIT,
        name="attend_backward",
    )(
        near_rank, far_rank, to_vmem(near_post), to_vmem(up_far), q, k, v, probs,
        qkv_weight, qkv_weight, qkv_weight, to_vmem(far_post), inv, gain,
    )
    order = [c for half in plane for c in half]
    branch = lax.all_to_all(branch, "chan", 0, 0, axis_index_groups=[order], tiled=True)
    encoded = pack(enc_same, enc_far)
    encoded = spread(encoded)
    core = (lax.axis_index("pos") % 2).astype(jnp.int32).reshape(1)
    half = shape((GROUP // 2, width + HDIM), F32)
    keep, send = pl.pallas_call(
        sums_kernel,
        in_specs=[smem] * 3 + [vmem] * 3,
        out_specs=[vmem] * 2,
        out_shape=[half] * 2,
        cost_estimate=cost(2 * rows * rows * width, 4 << 20),
        name="sums",
    )(core, near_rank, far_rank, to_vmem(part), to_vmem(branch), tokens)
    ranks = range(lax.axis_size("pos"))

    def swap(x, bit):
        return lax.ppermute(x, "pos", [(p, p ^ bit) for p in ranks])

    total = keep + swap(send, 1)
    total = (total + swap(total, 2)) + (swap(total, 4) + swap(total, 6))
    embed_grad, mix_grad = pl.pallas_call(
        final_kernel,
        in_specs=[smem] + [vmem] * 2,
        out_specs=[vmem] * 2,
        out_shape=[shape((GROUP, width), F32), shape((GROUP, GROUP), F32)],
        name="final",
    )(core, to_vmem(total), to_vmem(swap(total, 1)))
    tok_grad = pl.pallas_call(
        weight_kernel,
        in_specs=[smem] * 2 + [vmem] * 6,
        out_specs=vmem,
        out_shape=shape((pix, width), F32),
        cost_estimate=cost(8 * rows * pix * width, 4 << 20),
        name="weight",
    )(near_rank, far_rank, mixing, up_same, up_other, branch, pix_same, pix_other)
    encoded = pl.pallas_call(
        place_kernel,
        in_specs=[smem] * 2 + [vmem],
        out_specs=vmem,
        out_shape=shape((count, GROUP, width), BF16),
        cost_estimate=cost(0, 4 << 20),
        name="place",
    )(near, far, to_vmem(encoded))
    return (
        encoded.reshape(count, 1, GROUP, width),
        tok_grad.reshape(1, 1, pix, width),
        mix_grad.reshape(1, GROUP, GROUP),
        embed_grad,
    )


def solution(mesh):
    in_specs = (
        P(None, "pos", "chan", None),
        P("chan", None, None),
        P("chan", None, None),
        P("chan", None),
        P(),
        P(),
        P(None, "pos", "chan", None),
    )
    out_specs = (
        P(None, "pos", "chan", None),
        P("pos", "chan", None, None),
        P("chan", None, None),
        P("chan", None),
    )
    return jax.shard_map(step, mesh=mesh, in_specs=in_specs, out_specs=out_specs, check_vma=False)
```

```python
import math

import jax
import jax.numpy as jnp
from jax import lax
from jax.experimental import pallas as pl
from jax.experimental.pallas import tpu as pltpu
from jax.sharding import PartitionSpec as P


GROUP = 16
HEADS = 8
HDIM = 128
PAIR = 2 * HDIM
EPS = 1e-06
SCALE = 1.0 / math.sqrt(HDIM)
X, HALVES, Y = 4, 2, 4
PLANE = X * Y
BASE = [x * HALVES * Y + y for x in range(X) for y in range(Y)]
LIMIT = pltpu.CompilerParams(vmem_limit_bytes=57 << 20)
F32 = jnp.float32
BF16 = jnp.bfloat16


def nn(a, b):
    return jnp.dot(a, b, preferred_element_type=F32)


def nt(a, b):
    return lax.dot_general(a, b, (((1,), (1,)), ((), ())), preferred_element_type=F32)


def block_diagonal(small, size):
    rows = lax.broadcasted_iota(jnp.int32, (size, GROUP), 0)
    cols = lax.broadcasted_iota(jnp.int32, (size, GROUP), 1)
    pick = (rows % GROUP == cols).astype(BF16)
    tiled = nt(nn(pick, small).astype(BF16), pick)
    same = (
        lax.broadcasted_iota(jnp.int32, (size, size), 0) // GROUP
        == lax.broadcasted_iota(jnp.int32, (size, size), 1) // GROUP
    )
    return jnp.where(same, tiled, 0.0).astype(BF16), pick


def mix_block(start, patches_ref, weight_ref, mixing_ref, embed_ref, tokens_ref):
    pixels = jnp.concatenate([patches_ref[base + start] for base in BASE], axis=0)
    tokens = nn(pixels, weight_ref[...]).astype(BF16)
    tokens_ref[...] = tokens
    diag, pick = block_diagonal(mixing_ref[...], tokens.shape[0])
    mixed = (nn(diag, tokens) + nn(pick, embed_ref[...])).astype(BF16)
    return mixed.reshape(PLANE, GROUP, -1)


def mix_kernel(start_ref, patches_ref, weight_ref, mixing_ref, embed_ref, tokens_ref, mixed_ref):
    mixed_ref[...] = mix_block(
        start_ref[0], patches_ref, weight_ref, mixing_ref, embed_ref, tokens_ref
    )


def mix_near_kernel(
    near_at, far_at, patches_ref, weight_ref, mixing_ref, embed_ref, upstream_ref,
    tokens_ref, sent_ref,
):
    for k, base in enumerate(BASE):
        sent_ref[k, GROUP : 2 * GROUP] = upstream_ref[base + near_at[0]]
        sent_ref[k, 2 * GROUP :] = upstream_ref[base + far_at[0]]
    sent_ref[:, :GROUP] = mix_block(
        near_at[0], patches_ref, weight_ref, mixing_ref, embed_ref, tokens_ref
    )


def pack_kernel(same_ref, other_ref, both_ref):
    both_ref[:, :GROUP] = same_ref[...]
    both_ref[:, GROUP:] = other_ref[...]


def split_kernel(same_at, other_at, upstream_ref, same_ref, other_ref):
    for k, base in enumerate(BASE):
        same_ref[k] = upstream_ref[base + same_at[0]]
        other_ref[k] = upstream_ref[base + other_at[0]]


def place_kernel(same_at, other_at, both_ref, out_ref):
    for k, base in enumerate(BASE):
        out_ref[base + same_at[0]] = both_ref[k, :GROUP]
        out_ref[base + other_at[0]] = both_ref[k, GROUP:]


def forward_kernel(
    near_ref, far_ref, gain_ref, wq_ref, wk_ref, wv_ref,
    first_ref, second_ref, q_ref, k_ref, v_ref, probs_ref, inv_ref, normed_ref,
):
    step = pl.program_id(0)
    half = first_ref.shape[0]

    @pl.when(step == 0)
    def _():
        for ref, at in ((near_ref, 0), (far_ref, half)):
            mixed = ref[:, :GROUP].reshape(half, -1).astype(F32)
            inv = lax.rsqrt(jnp.mean(mixed * mixed, axis=-1, keepdims=True) + EPS)
            inv_ref[at : at + half] = inv
            normed_ref[at : at + half] = (mixed * inv * gain_ref[...]).astype(BF16)

    normed = normed_ref[...]
    q_ref[...] = nn(normed, wq_ref[...]).astype(BF16)
    k_ref[...] = nn(normed, wk_ref[...]).astype(BF16)
    v_ref[...] = nn(normed, wv_ref[...]).astype(BF16)
    spans = [slice(i * HDIM, (i + 1) * HDIM) for i in range(2)]
    scores = [nt(k_ref[:, cols], q_ref[:, cols]) for cols in spans]
    values = [v_ref[:, cols].T for cols in spans]
    for i, cols in enumerate(spans):
        peak = jnp.max(scores[i], axis=0, keepdims=True)
        exps = jnp.exp2((scores[i] - peak) * (SCALE * math.log2(math.e)))
        probs = exps * (1.0 / jnp.sum(exps, axis=0, keepdims=True))
        probs_ref[i] = probs
        attended = nn(values[i], probs.astype(BF16)).astype(BF16).T
        here = pl.ds(pl.multiple_of(step * PAIR, PAIR) + i * HDIM, HDIM)
        for ref, out_ref, at in ((near_ref, first_ref, 0), (far_ref, second_ref, half)):
            base = ref[:, :GROUP, here].reshape(half, HDIM).astype(F32)
            out_ref[:, cols] = (base + attended[at : at + half].astype(F32)).astype(BF16)


def backward_kernel(
    near_at, far_at,
    near_ref, up_far_ref, q_ref, k_ref, v_ref, probs_ref, wq_ref, wk_ref, wv_ref,
    far_ref, inv_ref, gain_ref, branch_ref, gq_ref, gk_ref, gv_ref, acc_ref,
):
    step = pl.program_id(0)
    half = acc_ref.shape[0] // 2
    for i in range(2):
        cols = slice(i * HDIM, (i + 1) * HDIM)
        here = pl.ds(pl.multiple_of(step * PAIR, PAIR) + i * HDIM, HDIM)
        up = jnp.concatenate(
            [
                near_ref[:, GROUP : 2 * GROUP, here].reshape(half, HDIM),
                up_far_ref[:, :, here].reshape(half, HDIM),
            ],
            axis=0,
        )
        probs = probs_ref[i]
        grad_probs = nt(v_ref[:, cols], up)
        inner = jnp.sum(probs * grad_probs, axis=0, keepdims=True)
        grad_scores = (probs * (grad_probs - inner) * SCALE).astype(BF16)
        gv_ref[:, cols] = nn(probs.astype(BF16), up).astype(BF16)
        gk_ref[:, cols] = nn(grad_scores, q_ref[:, cols]).astype(BF16)
        gq_ref[:, cols] = nn(k_ref[:, cols].T, grad_scores).astype(BF16).T
    grad = (
        nt(gq_ref[...], wq_ref[...]) + nt(gk_ref[...], wk_ref[...]) + nt(gv_ref[...], wv_ref[...])
    )

    @pl.when(step == 0)
    def _():
        acc_ref[...] = grad

    @pl.when(step > 0)
    def _():
        acc_ref[...] += grad

    @pl.when(step == pl.num_programs(0) - 1)
    def _():
        for ref, to, at in ((near_ref, near_at, 0), (far_ref, far_at, half)):
            scaled = acc_ref[at : at + half] * gain_ref[...]
            mixed = ref[:, :GROUP].reshape(half, -1).astype(F32)
            inv = inv_ref[at : at + half]
            mean = jnp.mean(scaled * mixed, axis=-1, keepdims=True)
            branch = (inv * (scaled - mixed * (inv * inv * mean))).astype(BF16)
            branch_ref[pl.ds(to[0], PLANE)] = branch.reshape(PLANE, GROUP, -1)


def partial_sums(rows, tokens):
    count, _, width = rows.shape
    size = count * GROUP
    embed = jnp.sum(rows.astype(F32), axis=0)
    same = (
        lax.broadcasted_iota(jnp.int32, (size, size), 0) // GROUP
        == lax.broadcasted_iota(jnp.int32, (size, size), 1) // GROUP
    )
    prods = jnp.where(same, nt(rows.reshape(size, width), tokens), 0.0)
    folded = jnp.sum(prods.reshape(count, GROUP, size), axis=0)
    folded = folded[:, :HDIM] + folded[:, HDIM:]
    for shift in (64, 32, 16):
        folded = folded + pltpu.roll(folded, shift, 1)
    return jnp.concatenate([embed, folded], axis=1)


def side_kernel(
    same_at, other_at, up_same_ref, up_other_ref, tok_same_ref, tok_other_ref, patches_ref,
    part_ref, pix_same_ref, pix_other_ref, tokens_ref,
):
    tokens_ref[: tok_same_ref.shape[0]] = tok_same_ref[...]
    tokens_ref[tok_same_ref.shape[0] :] = tok_other_ref[...]
    part_ref[...] = partial_sums(up_same_ref[...], tok_same_ref[...]) + partial_sums(
        up_other_ref[...], tok_other_ref[...]
    )
    for at, pixels_ref in ((same_at, pix_same_ref), (other_at, pix_other_ref)):
        start = at[0]
        pixels_ref[...] = jnp.concatenate([patches_ref[base + start] for base in BASE], axis=0).T


def sums_kernel(
    core_ref, near_at, far_at, part_ref, branch_ref, tokens_ref, keep_ref, send_ref
):
    both = part_ref[...]
    size = PLANE * GROUP
    for i, at in enumerate((near_at, far_at)):
        tokens = tokens_ref[i * size : (i + 1) * size]
        both += partial_sums(branch_ref[pl.ds(at[0], PLANE)], tokens)
    half = GROUP // 2
    first = core_ref[0] == 0
    keep_ref[...] = jnp.where(first, both[:half], both[half:])
    send_ref[...] = jnp.where(first, both[half:], both[:half])


def weight_kernel(
    near_at, far_at, mixing_ref, up_same_ref, up_other_ref, branch_ref, pix_same_ref,
    pix_other_ref, out_ref,
):
    size = pix_same_ref.shape[1]
    width = out_ref.shape[1]
    diag, _ = block_diagonal(mixing_ref[...], size)
    diag_t = diag.T
    total = None
    for at, up_ref, pixels_ref in (
        (near_at, up_same_ref, pix_same_ref), (far_at, up_other_ref, pix_other_ref)
    ):
        up = up_ref[...].reshape(size, width)
        branch = branch_ref[pl.ds(at[0], PLANE)].reshape(size, width)
        grad_tokens = (nn(diag_t, up) + nn(diag_t, branch)).astype(BF16)
        part = nn(pixels_ref[...], grad_tokens)
        total = part if total is None else total + part
    out_ref[...] = total


def final_kernel(core_ref, mine_ref, other_ref, embed_ref, mix_ref):
    half = GROUP // 2
    width = embed_ref.shape[1]
    first = core_ref[0] == 0
    mine = mine_ref[...]
    other = other_ref[...]
    low = jnp.where(first, mine, other)
    high = jnp.where(first, other, mine)
    embed_ref[:half, :] = low[:, :width]
    embed_ref[half:, :] = high[:, :width]
    mix_ref[:half, :] = low[:, width : width + GROUP]
    mix_ref[half:, :] = high[:, width : width + GROUP]


def to_vmem(x):
    return pltpu.with_memory_space_constraint(x, pltpu.VMEM)


def whole(shape):
    return pl.BlockSpec(shape, lambda *_: (0,) * len(shape))


def shape(dims, dtype):
    return jax.ShapeDtypeStruct(dims, dtype)


def cost(flops, read):
    return pl.CostEstimate(flops=flops, bytes_accessed=read, transcendentals=0)


def step(patches, tok_weight, mixing, chan_embed, norm_gain, qkv_weight, upstream):
    count = patches.shape[0]
    pix = patches.shape[3]
    width = tok_weight.shape[2]
    rows = PLANE * GROUP
    chans = lax.axis_size("chan") * GROUP
    steps = width // PAIR
    patches = patches.reshape(count, GROUP, pix)
    tok_weight = tok_weight.reshape(pix, width)
    mixing = mixing.reshape(GROUP, GROUP)
    upstream = upstream.reshape(count, GROUP, width)
    gain = norm_gain.reshape(1, width)
    vmem = pl.BlockSpec(memory_space=pltpu.VMEM)
    smem = pl.BlockSpec(memory_space=pltpu.SMEM)
    near = ((lax.axis_index("chan") // Y) % HALVES * Y).astype(jnp.int32).reshape(1)
    far = Y - near
    plane = [[base + h * Y for base in BASE] for h in range(HALVES)]
    piece = shape((PLANE, GROUP, width), BF16)

    def spread(x):
        x = x.reshape(PLANE, -1, width)
        return lax.all_to_all(x, "chan", 0, 0, axis_index_groups=plane, tiled=True)

    def flip(x):
        pairs = [(c, c ^ Y) for c in range(lax.axis_size("chan"))]
        return lax.ppermute(x.reshape(PLANE, GROUP, width), "chan", pairs)

    near_rank, far_rank = near // Y * PLANE, far // Y * PLANE

    tok_other, mixed_far = pl.pallas_call(
        mix_kernel,
        in_specs=[smem] + [vmem] * 4,
        out_specs=[vmem] * 2,
        out_shape=[shape((rows, width), BF16), piece],
        cost_estimate=cost(4 * rows * pix * width, 4 * rows * width),
        name="mix_other",
    )(far, patches, tok_weight, mixing, chan_embed)
    mixed_far = flip(mixed_far)
    tok_same, sent = pl.pallas_call(
        mix_near_kernel,
        in_specs=[smem] * 2 + [vmem] * 5,
        out_specs=[vmem] * 2,
        out_shape=[shape((rows, width), BF16), shape((PLANE, 3 * GROUP, width), BF16)],
        cost_estimate=cost(4 * rows * pix * width, 4 * rows * width),
        name="mix_same",
    )(near, far, patches, tok_weight, mixing, chan_embed, upstream)
    near_post = spread(sent)
    up_same, up_other = pl.pallas_call(
        split_kernel,
        in_specs=[smem] * 2 + [vmem],
        out_specs=[vmem] * 2,
        out_shape=[piece] * 2,
        cost_estimate=cost(0, 4 << 20),
        name="split",
    )(near, far, upstream)
    part, pix_same, pix_other, tokens = pl.pallas_call(
        side_kernel,
        in_specs=[smem] * 2 + [vmem] * 5,
        out_specs=[vmem] * 4,
        out_shape=[shape((GROUP, width + HDIM), F32)]
        + [shape((pix, rows), BF16)] * 2
        + [shape((chans, width), BF16)],
        cost_estimate=cost(4 * rows * rows * width, 4 << 20),
        name="side",
    )(near, far, up_same, up_other, tok_same, tok_other, patches)
    up_far = flip(near_post[:, 2 * GROUP :])
    mixed_far = spread(mixed_far)
    column = lambda part: pl.BlockSpec((width, PAIR), lambda i: (0, part * steps + i))
    heads = pl.BlockSpec((chans, PAIR), lambda i: (0, i))
    half_heads = pl.BlockSpec((rows, PAIR), lambda i: (0, i))
    pairs = pl.BlockSpec((2, chans, chans), lambda i: (i, 0, 0))
    enc_same, enc_other, q, k, v, probs, inv = pl.pallas_call(
        forward_kernel,
        grid=(steps,),
        in_specs=[vmem, vmem, whole((1, width)), column(0), column(1), column(2)],
        out_specs=[half_heads, half_heads, heads, heads, heads, pairs, whole((chans, 1))],
        out_shape=[shape((rows, width), BF16)] * 2
        + [shape((chans, width), BF16)] * 3
        + [shape((HEADS, chans, chans), F32), shape((chans, 1), F32)],
        scratch_shapes=[pltpu.VMEM((chans, width), BF16)],
        cost_estimate=cost(6 * chans * width * width + 4 * chans * chans * width, 16 << 20),
        name="attend_forward",
    )(to_vmem(near_post), to_vmem(mixed_far), gain, qkv_weight, qkv_weight, qkv_weight)
    enc_far = flip(enc_other)
    branch = pl.pallas_call(
        backward_kernel,
        grid=(steps,),
        in_specs=[smem] * 2
        + [vmem, vmem]
        + [heads] * 3
        + [pairs, column(0), column(1), column(2), vmem]
        + [whole((chans, 1)), whole((1, width))],
        out_specs=whole((count, GROUP, width)),
        out_shape=shape((count, GROUP, width), BF16),
        scratch_shapes=[pltpu.VMEM((chans, PAIR), BF16)] * 3 + [pltpu.VMEM((chans, width), F32)],
        cost_estimate=cost(6 * chans * width * width + 8 * chans * chans * width, 16 << 20),
        compiler_params=LIMIT,
        name="attend_backward",
    )(
        near_rank, far_rank, to_vmem(near_post), to_vmem(up_far), q, k, v, probs,
        qkv_weight, qkv_weight, qkv_weight, to_vmem(mixed_far), inv, gain,
    )
    order = [c for half in plane for c in half]
    branch = lax.all_to_all(branch, "chan", 0, 0, axis_index_groups=[order], tiled=True)
    double = shape((PLANE, 2 * GROUP, width), BF16)
    encoded = pl.pallas_call(
        pack_kernel,
        in_specs=[vmem] * 2,
        out_specs=vmem,
        out_shape=double,
        cost_estimate=cost(0, 4 << 20),
        compiler_params=LIMIT,
        name="pack",
    )(enc_same.reshape(piece.shape), enc_far)
    encoded = spread(encoded)
    core = (lax.axis_index("pos") % 2).astype(jnp.int32).reshape(1)
    half = shape((GROUP // 2, width + HDIM), F32)
    keep, send = pl.pallas_call(
        sums_kernel,
        in_specs=[smem] * 3 + [vmem] * 3,
        out_specs=[vmem] * 2,
        out_shape=[half] * 2,
        cost_estimate=cost(2 * rows * rows * width, 4 << 20),
        compiler_params=LIMIT,
        name="sums",
    )(core, near_rank, far_rank, to_vmem(part), to_vmem(branch), to_vmem(tokens))
    ranks = range(lax.axis_size("pos"))

    def swap(x, bit):
        return lax.ppermute(x, "pos", [(p, p ^ bit) for p in ranks])

    total = keep + swap(send, 1)
    total = (total + swap(total, 2)) + (swap(total, 4) + swap(total, 6))
    embed_grad, mix_grad = pl.pallas_call(
        final_kernel,
        in_specs=[smem] + [vmem] * 2,
        out_specs=[vmem] * 2,
        out_shape=[shape((GROUP, width), F32), shape((GROUP, GROUP), F32)],
        name="final",
    )(core, to_vmem(total), to_vmem(swap(total, 1)))
    tok_grad = pl.pallas_call(
        weight_kernel,
        in_specs=[smem] * 2 + [vmem] * 6,
        out_specs=vmem,
        out_shape=shape((pix, width), F32),
        cost_estimate=cost(8 * rows * pix * width, 4 << 20),
        name="weight",
    )(near_rank, far_rank, mixing, up_same, up_other, to_vmem(branch), pix_same, pix_other)
    encoded = pl.pallas_call(
        place_kernel,
        in_specs=[smem] * 2 + [vmem],
        out_specs=vmem,
        out_shape=shape((count, GROUP, width), BF16),
        cost_estimate=cost(0, 4 << 20),
        name="place",
    )(near, far, to_vmem(encoded))
    return (
        encoded.reshape(count, 1, GROUP, width),
        tok_grad.reshape(1, 1, pix, width),
        mix_grad.reshape(1, GROUP, GROUP),
        embed_grad,
    )


def solution(mesh):
    in_specs = (
        P(None, "pos", "chan", None),
        P("chan", None, None),
        P("chan", None, None),
        P("chan", None),
        P(),
        P(),
        P(None, "pos", "chan", None),
    )
    out_specs = (
        P(None, "pos", "chan", None),
        P("pos", "chan", None, None),
        P("chan", None, None),
        P("chan", None),
    )
    return jax.shard_map(step, mesh=mesh, in_specs=in_specs, out_specs=out_specs, check_vma=False)
```
